256 devices in a mesh: sample: 8 (over y_lo, x), seq: 16 (over y_hi, z), head: 2 (over core).
Axes of the slice: x: 4, y: 4 (y_hi: 2, y_lo: 2; y = y_hi * 2 + y_lo), z: 8, core: 2. Of those that a mesh axis runs over, the one named last changes fastest.
Arguments:
- values: bfloat16 [8, 8192, 4096], P('sample', 'seq', 'head'), may hold values from -6 to 6
- gate_values: bfloat16 [8, 8192, 4096], P('sample', 'seq', 'head'), may hold values from -6 to 6
- state_in: bfloat16 [8, 8192, 128], P('sample', 'seq'), may hold values from -0.5 to 0.5
- state_out: bfloat16 [8, 8192, 128], P('sample', 'seq'), may hold values from -0.5 to 0.5
- step_size: float32 [8, 8192, 64], P('sample', 'seq', 'head'), may hold values from 0.25 to 1
- log_decay: float32 [8, 8192, 64], P('sample', 'seq', 'head'), may hold values from -1 to 0, as said below
- skip_gain: float32 [64], P('head'), may hold values from 0.5 to 1.5
- norm_gain: float32 [4096], P('head'), may hold values from 0.25 to 1.75
- out_weight: bfloat16 [4096, 4096], P('head', 'seq'), may hold values from -0.09375 to 0.09375
- prompt_state: float32 [64, 64, 128], P('head', None, 'sample'), may hold values from -16 to 16
Outputs:
- projected: bfloat16 [8, 8192, 4096], P('sample', 'seq', 'head')
The draws below stay inside these ranges and needn't reach their ends.
Inputs may be any that keep to these rules, and one draw needn't show every extreme that they name: `log_decay`: every entry is negative.
All inputs are finite; a program needn't handle non-finite values.
Results may differ from the reference program's by a relative error of at most 0.019.
Values may be sent and summed in bfloat16 or wider, within the bound.
A program may use at most 128 MiB of HBM per device.

```python
import math
import jax
import jax.numpy as jnp
from jax import lax

STATE_HEADS = 64
P_SIZE = 64
N = 128
DO = 4096
L = 256
GROUP_HEADS = 8
TOK_DEV = 512
HP = 4096
SAMPLE_COUNT = 8
SAMPLE_LENGTH = 8192
N_HEAD = 2


def draw_log_decay(key, part):
    random_rapid_key, random_brisk_key, random_gradual_key, random_block_key, random_token_key, random_spike_key, random_magnitude_key = jax.random.split(key, 7)
    fast_share = 0.5
    is_fast = jax.random.bernoulli(random_rapid_key, fast_share, (1, 1, STATE_HEADS))
    quick_rate = jax.random.uniform(random_brisk_key, (1, 1, STATE_HEADS), jnp.float32, 0.04, 0.08)
    slow_rate = jax.random.uniform(random_gradual_key, (1, 1, STATE_HEADS), jnp.float32, 0.05, 0.35) / SAMPLE_LENGTH
    baseline_decay_rate = jnp.where(is_fast, quick_rate, slow_rate)
    blocks = SAMPLE_LENGTH // TOK_DEV
    multiplier = jnp.exp(jax.random.uniform(random_block_key, (SAMPLE_COUNT, blocks, 1, STATE_HEADS), jnp.float32, -0.6931, 0.6931))
    multiplier = jnp.broadcast_to(multiplier, (SAMPLE_COUNT, blocks, TOK_DEV, STATE_HEADS)).reshape(SAMPLE_COUNT, SAMPLE_LENGTH, STATE_HEADS)
    jitter_amplitude = jax.random.uniform(random_token_key, (SAMPLE_COUNT, SAMPLE_LENGTH, STATE_HEADS), jnp.float32, 0.5, 1.5)
    spike_position = jax.random.randint(random_spike_key, (SAMPLE_COUNT, 2), 0, SAMPLE_LENGTH)
    token_offset = jnp.arange(SAMPLE_LENGTH)
    spike_row_indices = jnp.any(token_offset[None, :, None] == spike_position[:, None, :], axis=2)
    spike_magnitude = jax.random.uniform(random_magnitude_key, (SAMPLE_COUNT, SAMPLE_LENGTH, STATE_HEADS), jnp.float32, 0.22, 0.51)
    return -(baseline_decay_rate * multiplier * jitter_amplitude) - spike_row_indices[:, :, None].astype(jnp.float32) * spike_magnitude


def shard_levels(rng, shape, cuts, low, largest):
    level = 1.0
    for axis_at, parts in cuts:
        heights = jax.random.uniform(jax.random.fold_in(jax.random.fold_in(rng, 6), axis_at), (parts,), jnp.float32, low / len(cuts), largest / len(cuts))
        level = level * jnp.repeat(jnp.exp(heights), shape[axis_at] // parts).reshape((-1,) + (1,) * (len(shape) - 1 - axis_at))
    return level


def bell_draw(rng, dims, scale, reach, cuts=(), dtype=jnp.bfloat16):
    drawn = jax.random.normal(rng, dims, jnp.float32) * scale
    if len(cuts) > 0:
        drawn = shard_levels(rng, dims, cuts, -0.22, 0.18) * drawn
    return jnp.clip(drawn, min=-reach, max=reach).astype(dtype)


def setup_inputs(seed: int = 0) -> dict:
    key_list = jax.random.split(jax.random.key(seed), 11)
    return {
        "values": bell_draw(key_list[0], (SAMPLE_COUNT, SAMPLE_LENGTH, HP), 1.0, 6.0, ((0, 8), (1, 16), (2, 2))),
        "gate_values": bell_draw(key_list[1], (SAMPLE_COUNT, SAMPLE_LENGTH, HP), 1.0, 6.0, ((0, 8), (1, 16), (2, 2))),
        "state_in": bell_draw(key_list[2], (SAMPLE_COUNT, SAMPLE_LENGTH, N), N ** -0.5, 0.5, ((0, 8), (1, 16))),
        "state_out": bell_draw(key_list[3], (SAMPLE_COUNT, SAMPLE_LENGTH, N), N ** -0.5, 0.5, ((0, 8), (1, 16))),
        "step_size": jnp.clip(jnp.exp(math.log(1.0) - 1.3862944 * jax.random.uniform(key_list[4], (SAMPLE_COUNT, SAMPLE_LENGTH, STATE_HEADS), jnp.float32) ** shard_levels(key_list[4], (SAMPLE_COUNT, SAMPLE_LENGTH, STATE_HEADS), ((0, 8), (1, 16), (2, 2)), -0.2, 0.2)), 0.25, 1.0),
        "log_decay": draw_log_decay(jax.random.fold_in(key_list[10], 71), 0),
        "skip_gain": jnp.clip(0.5 + 1.0 * jax.random.uniform(key_list[6], (STATE_HEADS,), jnp.float32) ** shard_levels(key_list[6], (STATE_HEADS,), ((0, 2),), -0.2, 0.2), 0.5, 1.5),
        "norm_gain": jnp.clip(1.0 + 0.15 * jax.random.normal(key_list[7], (HP,), jnp.float32), 0.25, 1.75),
        "out_weight": bell_draw(key_list[8], (HP, DO), HP ** -0.5, 0.09375, ((0, 2), (1, 16))),
        "prompt_state": bell_draw(key_list[9], (STATE_HEADS, P_SIZE, N), 3.0, 16.0, ((0, 2), (2, 8)), jnp.float32),
    }


EPSILON = 1e-05

def block_terms(values_blk, in_blk, out_blk, step_blk, decay_blk, skip_gain):
    heads = decay_blk.shape[1]
    running = jnp.cumsum(decay_blk, axis=0)
    per_head = values_blk.reshape(values_blk.shape[0], heads, -1)
    scaled = (per_head.astype(jnp.float32) * step_blk[:, :, None]).astype(jnp.bfloat16)
    scores = jnp.dot(out_blk, in_blk.T, preferred_element_type=jnp.float32)
    token_offset = jnp.arange(values_blk.shape[0])
    causal = token_offset[:, None] >= token_offset[None, :]
    by_head = running.T
    spread = by_head[:, :, None] - by_head[:, None, :]
    pair_decay = jnp.exp(jnp.where(causal[None], spread, -1e+30))
    mixing = (scores[None] * pair_decay).astype(jnp.bfloat16)
    inner = jnp.einsum('hts,shp->thp', mixing.astype(jnp.float32), scaled.astype(jnp.float32), precision=lax.Precision.HIGHEST)
    tail = jnp.exp(running[-1][None, :] - running)
    weighted = (scaled.astype(jnp.float32) * tail[:, :, None]).astype(jnp.bfloat16)
    block_state = jnp.einsum('shp,sn->hpn', weighted.astype(jnp.float32), in_blk.astype(jnp.float32), precision=lax.Precision.HIGHEST)
    local_out = inner + skip_gain[None, :, None] * per_head.astype(jnp.float32)
    return (local_out, running, block_state)

def group_norm(gated, norm_gain):
    width = GROUP_HEADS * P_SIZE
    grouped = gated.reshape(gated.shape[0], -1, width)
    mean_square = lax.optimization_barrier(jnp.mean(grouped * grouped, axis=-1, keepdims=True))
    rescaled = grouped * lax.rsqrt(mean_square + EPSILON)
    return (rescaled.reshape(gated.shape) * norm_gain).astype(jnp.bfloat16)

def reference(values, gate_values, state_in, state_out, step_size, log_decay, skip_gain, norm_gain, out_weight, prompt_state):
    count = SAMPLE_LENGTH // L

    def one_sample(inputs):
        values_s, gate_s, in_s, out_s, step_s, decay_s = inputs
        blocks = (values_s.reshape(count, L, -1), in_s.reshape(count, L, -1), out_s.reshape(count, L, -1), step_s.reshape(count, L, -1), decay_s.reshape(count, L, -1))

        def advance(state, block):
            values_blk, in_blk, out_blk, step_blk, decay_blk = block
            local_out, running, block_state = block_terms(values_blk, in_blk, out_blk, step_blk, decay_blk, skip_gain)
            state_low = state.astype(jnp.bfloat16).astype(jnp.float32)
            carried = jnp.exp(running)[:, :, None] * jnp.einsum('tn,hpn->thp', out_blk.astype(jnp.float32), state_low, precision=lax.Precision.HIGHEST)
            new_state = jnp.exp(running[-1])[:, None, None] * state + block_state
            return (new_state, local_out + carried)
        final_state, outputs = lax.scan(advance, prompt_state, blocks)
        outputs = outputs.reshape(SAMPLE_LENGTH, HP)
        gated = outputs * jax.nn.silu(gate_s.astype(jnp.float32))
        normed = group_norm(gated, norm_gain)
        rows = HP // N_HEAD
        total = jnp.zeros((SAMPLE_LENGTH, DO), jnp.float32)
        for shard in range(N_HEAD):
            partial_sum = jnp.dot(normed[:, shard * rows:(shard + 1) * rows], out_weight[shard * rows:(shard + 1) * rows], preferred_element_type=jnp.float32)
            partial_sum = lax.optimization_barrier(partial_sum.astype(jnp.bfloat16))
            total = total + partial_sum.astype(jnp.float32)
        return total.astype(jnp.bfloat16)
    return lax.map(one_sample, (values, gate_values, state_in, state_out, step_size, log_decay))
```

```python
from functools import partial

import jax
import jax.numpy as jnp
from jax import lax
from jax.experimental import pallas as pl
from jax.experimental.pallas import tpu as pltpu
from jax.sharding import Mesh
from jax.sharding import PartitionSpec as P

P_SIZE = 64
L = 256
GROUP_HEADS = 8
SEQ = ("yhi", "z")
SAMPLE = ("ylo", "x")
NZ = 8
MESH_ID = pl.DeviceIdType.MESH
EPSILON = 1e-05


def place():
    names = ("ylo", "x", "yhi", "z", "head")
    at = {name: lax.axis_index(name) for name in names}
    y = at["yhi"] * 2 + at["ylo"]
    up, down = lax.rem(y + 1, 4), lax.rem(y + 3, 4)
    near = {
        "+x": {"x": lax.rem(at["x"] + 1, 4)},
        "-x": {"x": lax.rem(at["x"] + 3, 4)},
        "+y": {"yhi": up // 2, "ylo": lax.rem(up, 2)},
        "-y": {"yhi": down // 2, "ylo": lax.rem(down, 2)},
        "+z": {"z": lax.rem(at["z"] + 1, NZ)},
        "-z": {"z": lax.rem(at["z"] + NZ - 1, NZ)},
        "across": {"yhi": 1 - at["yhi"], "ylo": 1 - at["ylo"]},
        "sibling": {"head": 1 - at["head"]},
    }
    return at, near


WAYS = ("+x", "-x", "+y", "-y")


class Gather:
    def __init__(self, at, near, own, wbuf, sems):
        self.at, self.near, self.own, self.wbuf = at, near, own, wbuf
        self.zs, self.zr, self.fs, self.fr, self.gs, self.gr, self.ls = sems
        px, lo = lax.rem(at["x"], 2), at["ylo"]
        self.mine = px * 2 + lo
        self.byx = (1 - px) * 2 + lo
        self.byy = px * 2 + 1 - lo
        self.px = px
        self.s_own = at["yhi"] * NZ + at["z"]
        self.s_across = (1 - at["yhi"]) * NZ + at["z"]

    def copy(self, src, s, start, size, send, recv, to):
        dst = self.wbuf.at[s, pl.ds(start, size)]
        return pltpu.make_async_remote_copy(
            src_ref=dst if src is None else src,
            dst_ref=dst,
            send_sem=send,
            recv_sem=recv,
            device_id=self.near[to],
            device_id_type=MESH_ID,
        )

    def shard(self, fam, z):
        hi = self.at["yhi"] if fam == 0 else 1 - self.at["yhi"]
        return hi * NZ + lax.rem(z + 2 * NZ, NZ)

    def events(self, n):
        fam, k = n % 2, n // 2
        found = []
        if k < (4 if fam == 0 else 3):
            found.append((self.shard(fam, self.at["z"] - 1 - k), k, "+z"))
        if k < (3 if fam == 0 else 4):
            found.append((self.shard(fam, self.at["z"] + 1 + k), k, "-z"))
        return fam, found

    def ring(self, s, way, slot, src=None):
        return self.copy(src, s, self.mine * 4, 4, self.zs.at[slot], self.zr.at[s], way)

    def local(self):
        return pltpu.make_async_copy(self.own, self.wbuf.at[self.s_own], self.ls)

    def give(self):
        start = self.px * 8
        src = self.own.at[pl.ds(start, 8)]
        return self.copy(src, self.s_own, start, 8, self.zs.at[0], self.zr.at[self.s_own], "across")

    def given(self):
        start = self.px * 8
        return self.copy(None, self.s_across, start, 8, self.zs.at[0], self.zr.at[self.s_across], "across")

    def give_on(self, d):
        start = self.px * 8 + 4 * d
        return self.copy(
            None, self.s_across, start, 4, self.fs.at[0, d], self.fr.at[self.s_across, d], WAYS[d]
        )

    def given_on(self, d):
        start = (1 - self.px) * 8 + 4 * d
        return self.copy(
            None, self.s_across, start, 4, self.fs.at[0, d], self.fr.at[self.s_across, d], WAYS[d]
        )

    def first(self, s, d, slot):
        start = self.mine * 4 + 2 * (d % 2)
        return self.copy(None, s, start, 2, self.fs.at[slot, d], self.fr.at[s, d], WAYS[d])

    def first_in(self, s, d):
        start = (self.byx if d < 2 else self.byy) * 4 + 2 * (d % 2)
        return self.copy(None, s, start, 2, self.fs.at[0, d], self.fr.at[s, d], WAYS[d])

    def second(self, s, d, slot):
        start = (self.byy if d < 2 else self.byx) * 4 + (0, 2, 1, 3)[d]
        return self.copy(None, s, start, 1, self.gs.at[slot, d], self.gr.at[s, d], WAYS[d])

    def second_in(self, s, d):
        far = 3 - self.mine
        start = far * 4 + (0, 2, 1, 3)[d]
        return self.copy(None, s, start, 1, self.gs.at[0, d], self.gr.at[s, d], WAYS[d])

    def begin(self):
        src = self.own.at[pl.ds(self.mine * 4, 4)]
        self.sent = []
        for c in (
            self.ring(self.s_own, "+z", 1, src),
            self.ring(self.s_own, "-z", 2, src),
            self.give(),
        ):
            c.start()
            self.sent.append(c)
        self.local().start()
        self.slots = {"z": 3, "f": 1, "g": 0}

    def begin_across(self):
        self.given().wait_recv()
        for c in (
            self.ring(self.s_across, "+z", 3),
            self.ring(self.s_across, "-z", 4),
            self.give_on(0),
            self.give_on(1),
        ):
            c.start()
            self.sent.append(c)
        self.slots["z"] = 5

    def forward(self, n):
        fam, found = self.events(n)
        for s, k, way in found:
            self.ring(s, way, 0).wait_recv()
            last = k + 1 == ((4 if fam == 0 else 3) if way == "+z" else (3 if fam == 0 else 4))
            if not last:
                c = self.ring(s, way, self.slots["z"])
                self.slots["z"] += 1
                c.start()
                self.sent.append(c)
            for d in range(4):
                c = self.first(s, d, self.slots["f"])
                c.start()
                self.sent.append(c)
            self.slots["f"] += 1

    def spread(self, n):
        fam, found = self.events(n)
        for s, k, way in found:
            for d in (2, 3, 0, 1):
                self.first_in(s, d).wait_recv()
                c = self.second(s, (d + 2) % 4, self.slots["g"])
                c.start()
                self.sent.append(c)
            self.slots["g"] += 1

    def arrived(self, n):
        fam, found = self.events(n)
        for s, k, way in found:
            for d in range(4):
                self.second_in(s, d).wait_recv()

    def arrived_across(self):
        self.local().wait()
        for d in range(2):
            self.given_on(d).wait_recv()

    def finish(self):
        for c in self.sent:
            c.wait_send()


def greet(near, extra=()):
    barrier = pltpu.get_barrier_semaphore()
    who = [near[k] for k in ("+x", "-x", "+y", "-y", "+z", "-z", "sibling")] + list(extra)
    for device in who:
        pl.semaphore_signal(barrier, inc=1, device_id=device, device_id_type=MESH_ID)
    pl.semaphore_wait(barrier, len(who))


GATHER_SEMS = [
    pltpu.SemaphoreType.DMA((17,)),
    pltpu.SemaphoreType.DMA((16,)),
    pltpu.SemaphoreType.DMA((15, 4)),
    pltpu.SemaphoreType.DMA((16, 4)),
    pltpu.SemaphoreType.DMA((14, 4)),
    pltpu.SemaphoreType.DMA((16, 4)),
    pltpu.SemaphoreType.DMA,
]


class Project:
    def __init__(self, at, near, normed, wbuf, part, got, out, sems):
        self.at, self.near, self.normed, self.wbuf = at, near, normed, wbuf
        self.part, self.got, self.out, self.ss, self.rs = part, got, out, *sems

    def dot(self, s):
        w = self.wbuf[s].reshape(2048, 256)
        return jnp.dot(self.normed[...], w, preferred_element_type=jnp.float32).astype(jnp.bfloat16)

    def copy(self, z):
        return pltpu.make_async_remote_copy(
            src_ref=self.part.at[1, z],
            dst_ref=self.got.at[z],
            send_sem=self.ss.at[z],
            recv_sem=self.rs.at[z],
            device_id=self.near["sibling"],
            device_id_type=MESH_ID,
        )

    def columns(self, z):
        c = self.at["head"]
        self.part[1, z] = self.dot((1 - c) * NZ + z)
        self.copy(z).start()
        self.part[0, z] = self.dot(c * NZ + z)

    def combine(self, z):
        self.copy(z).wait_recv()
        total = self.part[0, z].astype(jnp.float32) + self.got[z].astype(jnp.float32)
        start = pl.multiple_of(z * 256, 256)
        self.out[:, pl.ds(start, 256)] = total.astype(jnp.bfloat16)


def gather_kernel(own, normed, out, wbuf, part, got, *sems):
    at, near = place()
    greet(near)
    gather = Gather(at, near, own, wbuf, sems[:7])
    proj = Project(at, near, normed, wbuf, part, got, out, sems[7:])
    z = at["z"]
    gather.begin()
    gather.forward(0)
    gather.begin_across()
    ready = {1: (1, 2), 3: (2, 3), 5: (3, 4), 7: (4, 5)}

    def columns(lo, hi):
        for k in range(lo, hi):
            proj.columns(lax.rem(z + k, NZ))
            if 0 < k < 4:
                proj.columns(lax.rem(z + NZ - k, NZ))

    gather.forward(1)
    gather.spread(0)
    gather.arrived_across()
    columns(0, 1)
    for n in range(2, 8):
        gather.forward(n)
        gather.spread(n - 1)
        gather.arrived(n - 2)
        if n % 2 == 1:
            k = (n - 1) // 2
            columns(k, k + 1)
    gather.spread(7)
    gather.arrived(6)
    gather.arrived(7)
    columns(4, 5)
    for k in range(NZ):
        proj.combine(k)
    for k in range(NZ):
        proj.copy(k).wait_send()
    gather.finish()


def project(normed, out_weight):
    own = out_weight.reshape(16, 128, 256)
    vmem = pl.BlockSpec(memory_space=pltpu.VMEM)
    return pl.pallas_call(
        gather_kernel,
        out_shape=jax.ShapeDtypeStruct((512, 2048), jnp.bfloat16),
        in_specs=[pl.BlockSpec(memory_space=pl.ANY), vmem],
        out_specs=vmem,
        scratch_shapes=[
            pltpu.VMEM((16, 16, 128, 256), jnp.bfloat16),
            pltpu.VMEM((2, NZ, 512, 256), jnp.bfloat16),
            pltpu.VMEM((NZ, 512, 256), jnp.bfloat16),
            *GATHER_SEMS,
            pltpu.SemaphoreType.DMA((NZ,)),
            pltpu.SemaphoreType.DMA((NZ,)),
        ],
        compiler_params=pltpu.CompilerParams(
            collective_id=0, has_side_effects=True, vmem_limit_bytes=48 << 20
        ),
    )(own, normed)


def neutral_like(array, identity):
    return jax.tree.map(
        lambda a, e: jnp.broadcast_to(jnp.asarray(e, a.dtype), a.shape), array, identity
    )


def entering(array, axes, combine, identity):
    before = start = neutral_like(array, identity)
    so_far = array
    for axis in reversed(axes):
        peers, index = (lax.axis_size(axis), lax.axis_index(axis))
        pieces = jax.tree.map(
            lambda part, kind: lax.all_gather(part.astype(kind), axis),
            so_far,
            (jnp.bfloat16, jnp.bfloat16),
        )
        inside, so_far = (start, start)
        for k in range(peers):
            passed = k < index
            so_far = combine(
                so_far, jax.tree.map(lambda part, own: part[k].astype(own.dtype), pieces, array)
            )
            inside = jax.tree.map(lambda new, old: jnp.where(passed, new, old), so_far, inside)
        before = combine(inside, before)
    return before


def in_blocks(array, dim, peers):
    dims = array.shape
    tiles = array.reshape(*dims[:dim], peers, dims[dim] // peers, *dims[dim + 1 :])
    return jnp.moveaxis(tiles, dim, 0)


def sent_and_summed(array, axis, dim):
    peers = lax.axis_size(axis)
    tiles = lax.all_to_all(in_blocks(array, dim, peers), axis, 0, 0, tiled=True)
    return jnp.sum(tiles.astype(jnp.float32), axis=0)


def block_terms(values_blk, in_blk, out_blk, step_blk, decay_blk, skip_gain):
    heads = decay_blk.shape[1]
    steps = jnp.arange(decay_blk.shape[0])
    lower = (steps[:, None] >= steps[None, :]).astype(jnp.float32)
    running = jnp.dot(lower, decay_blk, precision=lax.Precision.HIGHEST)
    per_head = values_blk.reshape(values_blk.shape[0], heads, -1)
    scaled = (per_head.astype(jnp.float32) * step_blk[:, :, None]).astype(jnp.bfloat16)
    scores = jnp.dot(out_blk, in_blk.T, preferred_element_type=jnp.float32)
    token_offset = jnp.arange(values_blk.shape[0])
    causal = token_offset[:, None] >= token_offset[None, :]
    by_head = running.T
    spread = by_head[:, :, None] - by_head[:, None, :]
    pair_decay = jnp.exp(jnp.where(causal[None], spread, -1e30))
    mixing = (scores[None] * pair_decay).astype(jnp.bfloat16)
    inner = jnp.einsum("hts,shp->thp", mixing, scaled, preferred_element_type=jnp.float32)
    tail = jnp.exp(running[-1][None, :] - running)
    weighted = (scaled.astype(jnp.float32) * tail[:, :, None]).astype(jnp.bfloat16)
    block_state = jnp.einsum("shp,sn->hpn", weighted, in_blk, preferred_element_type=jnp.float32)
    local_out = inner + skip_gain[None, :, None] * per_head.astype(jnp.float32)
    return (local_out, running, block_state)


def local_sweep(values_s, in_s, out_s, step_s, decay_s, skip_gain):
    count = values_s.shape[0] // L
    heads = decay_s.shape[1]
    width = values_s.shape[1] // heads
    states = in_s.shape[1]
    blocks = (
        values_s.reshape(count, L, -1),
        in_s.reshape(count, L, -1),
        out_s.reshape(count, L, -1),
        step_s.reshape(count, L, heads),
        decay_s.reshape(count, L, heads),
    )

    def advance(carry, block):
        state, total = carry
        values_blk, in_blk, out_blk, step_blk, decay_blk = block
        local_out, running, block_state = block_terms(
            values_blk, in_blk, out_blk, step_blk, decay_blk, skip_gain
        )
        new_state = jnp.exp(running[-1])[:, None, None] * state + block_state
        return ((new_state, total + running[-1]), (local_out, running, state, total))

    initial = (jnp.zeros((heads, width, states), jnp.float32), jnp.zeros((heads,), jnp.float32))
    return lax.scan(advance, initial, blocks)


def link(earlier, later):
    decay_early, state_early = earlier
    decay_late, state_late = later
    return (decay_early * decay_late, decay_late[:, :, None, None] * state_early + state_late)


def group_norm(gated, norm_gain):
    width = GROUP_HEADS * P_SIZE
    grouped = gated.reshape(gated.shape[0], -1, width)
    mean_square = jnp.mean(grouped * grouped, axis=-1, keepdims=True)
    rescaled = grouped * lax.rsqrt(mean_square + EPSILON)
    return (rescaled.reshape(gated.shape) * norm_gain).astype(jnp.bfloat16)


def shards(
    values,
    gate_values,
    state_in,
    state_out,
    step_size,
    log_decay,
    skip_gain,
    norm_gain,
    out_weight,
    prompt_state,
):
    prompt = lax.all_gather(prompt_state.astype(jnp.bfloat16), SAMPLE, axis=2, tiled=True).astype(
        prompt_state.dtype
    )
    sweep_sample = partial(local_sweep, skip_gain=skip_gain)
    (last_state, last_total), (local_out, running, before, totals) = jax.vmap(sweep_sample)(
        values, state_in, state_out, step_size, log_decay
    )
    identity = (jnp.ones_like(last_total), jnp.zeros_like(last_state))
    lead_decay, lead_state = entering((jnp.exp(last_total), last_state), SEQ, link, identity)
    entry = lead_state + lead_decay[:, :, None, None] * prompt[None]
    start = before + jnp.exp(totals)[:, :, :, None, None] * entry[:, None]
    start_low = start.astype(jnp.bfloat16)
    samples, tokens = (values.shape[0], values.shape[1])
    count = tokens // L
    out_blocks = state_out.reshape(samples, count, L, -1)
    carried = jnp.exp(running)[..., None] * jnp.einsum(
        "sktn,skhpn->skthp", out_blocks, start_low, preferred_element_type=jnp.float32
    )
    outputs = (local_out + carried).reshape(samples * tokens, -1)
    gated = outputs * jax.nn.silu(gate_values.reshape(samples * tokens, -1).astype(jnp.float32))
    normed = group_norm(gated, norm_gain)
    mine = project(normed, out_weight)
    return mine.reshape(samples, tokens, -1)


def solution(mesh):
    split = Mesh(
        mesh.devices.reshape(2, 4, 2, 8, 2),
        ("ylo", "x", "yhi", "z", "head"),
    )
    return jax.shard_map(
        shards,
        mesh=split,
        in_specs=(
            P(SAMPLE, SEQ, "head"),
            P(SAMPLE, SEQ, "head"),
            P(SAMPLE, SEQ, None),
            P(SAMPLE, SEQ, None),
            P(SAMPLE, SEQ, "head"),
            P(SAMPLE, SEQ, "head"),
            P("head"),
            P("head"),
            P("head", SEQ),
            P("head", None, SAMPLE),
        ),
        out_specs=P(SAMPLE, SEQ, "head"),
        check_vma=False,
    )
```

```python
from functools import partial

import jax
import jax.numpy as jnp
from jax import lax
from jax.experimental import pallas as pl
from jax.experimental.pallas import tpu as pltpu
from jax.sharding import Mesh
from jax.sharding import PartitionSpec as P

P_SIZE = 64
L = 256
GROUP_HEADS = 8
SEQ = ("yhi", "z")
SAMPLE = ("ylo", "x")
NZ = 8
MESH_ID = pl.DeviceIdType.MESH
EPSILON = 1e-05


def place():
    names = ("ylo", "x", "yhi", "z", "head")
    at = {name: lax.axis_index(name) for name in names}
    y = at["yhi"] * 2 + at["ylo"]
    up, down = lax.rem(y + 1, 4), lax.rem(y + 3, 4)
    near = {
        "+x": {"x": lax.rem(at["x"] + 1, 4)},
        "-x": {"x": lax.rem(at["x"] + 3, 4)},
        "+y": {"yhi": up // 2, "ylo": lax.rem(up, 2)},
        "-y": {"yhi": down // 2, "ylo": lax.rem(down, 2)},
        "+z": {"z": lax.rem(at["z"] + 1, NZ)},
        "-z": {"z": lax.rem(at["z"] + NZ - 1, NZ)},
        "across": {"yhi": 1 - at["yhi"], "ylo": 1 - at["ylo"]},
        "sibling": {"head": 1 - at["head"]},
    }
    return at, near


WAYS = ("+x", "-x", "+y", "-y")


class Gather:
    def __init__(self, at, near, own, wbuf, sems):
        self.at, self.near, self.own, self.wbuf = at, near, own, wbuf
        self.zs, self.zr, self.fs, self.fr, self.gs, self.gr, self.ls = sems
        px, lo = lax.rem(at["x"], 2), at["ylo"]
        self.mine = px * 2 + lo
        self.byx = (1 - px) * 2 + lo
        self.byy = px * 2 + 1 - lo
        self.px = px
        self.s_own = at["yhi"] * NZ + at["z"]
        self.s_across = (1 - at["yhi"]) * NZ + at["z"]

    def copy(self, src, s, start, size, send, recv, to):
        dst = self.wbuf.at[s, pl.ds(start, size)]
        return pltpu.make_async_remote_copy(
            src_ref=dst if src is None else src,
            dst_ref=dst,
            send_sem=send,
            recv_sem=recv,
            device_id=self.near[to],
            device_id_type=MESH_ID,
        )

    def shard(self, fam, z):
        hi = self.at["yhi"] if fam == 0 else 1 - self.at["yhi"]
        return hi * NZ + lax.rem(z + 2 * NZ, NZ)

    def events(self, n):
        fam, k = n % 2, n // 2
        found = []
        if k < (4 if fam == 0 else 3):
            found.append((self.shard(fam, self.at["z"] - 1 - k), k, "+z"))
        if k < (3 if fam == 0 else 4):
            found.append((self.shard(fam, self.at["z"] + 1 + k), k, "-z"))
        return fam, found

    def ring(self, s, way, slot, src=None):
        return self.copy(src, s, self.mine * 4, 4, self.zs.at[slot], self.zr.at[s], way)

    def local(self):
        return pltpu.make_async_copy(self.own, self.wbuf.at[self.s_own], self.ls)

    def give(self):
        start = self.px * 8
        src = self.own.at[pl.ds(start, 8)]
        return self.copy(src, self.s_own, start, 8, self.zs.at[0], self.zr.at[self.s_own], "across")

    def given(self):
        start = self.px * 8
        return self.copy(None, self.s_across, start, 8, self.zs.at[0], self.zr.at[self.s_across], "across")

    def give_on(self, d):
        start = self.px * 8 + 4 * d
        return self.copy(
            None, self.s_across, start, 4, self.fs.at[0, d], self.fr.at[self.s_across, d], WAYS[d]
        )

    def given_on(self, d):
        start = (1 - self.px) * 8 + 4 * d
        return self.copy(
            None, self.s_across, start, 4, self.fs.at[0, d], self.fr.at[self.s_across, d], WAYS[d]
        )

    def first(self, s, d, slot):
        start = self.mine * 4 + 2 * (d % 2)
        return self.copy(None, s, start, 2, self.fs.at[slot, d], self.fr.at[s, d], WAYS[d])

    def first_in(self, s, d):
        start = (self.byx if d < 2 else self.byy) * 4 + 2 * (d % 2)
        return self.copy(None, s, start, 2, self.fs.at[0, d], self.fr.at[s, d], WAYS[d])

    def second(self, s, d, slot):
        start = (self.byy if d < 2 else self.byx) * 4 + (0, 2, 1, 3)[d]
        return self.copy(None, s, start, 1, self.gs.at[slot, d], self.gr.at[s, d], WAYS[d])

    def second_in(self, s, d):
        far = 3 - self.mine
        start = far * 4 + (0, 2, 1, 3)[d]
        return self.copy(None, s, start, 1, self.gs.at[0, d], self.gr.at[s, d], WAYS[d])

    def begin(self):
        src = self.own.at[pl.ds(self.mine * 4, 4)]
        self.sent = []
        for c in (
            self.ring(self.s_own, "+z", 1, src),
            self.ring(self.s_own, "-z", 2, src),
            self.give(),
        ):
            c.start()
            self.sent.append(c)
        self.local().start()
        self.slots = {"z": 3, "f": 1, "g": 0}

    def begin_across(self):
        self.given().wait_recv()
        for c in (
            self.ring(self.s_across, "+z", 3),
            self.ring(self.s_across, "-z", 4),
            self.give_on(0),
            self.give_on(1),
        ):
            c.start()
            self.sent.append(c)
        self.slots["z"] = 5

    def forward(self, n):
        fam, found = self.events(n)
        for s, k, way in found:
            self.ring(s, way, 0).wait_recv()
            last = k + 1 == ((4 if fam == 0 else 3) if way == "+z" else (3 if fam == 0 else 4))
            if not last:
                c = self.ring(s, way, self.slots["z"])
                self.slots["z"] += 1
                c.start()
                self.sent.append(c)
            for d in range(4):
                c = self.first(s, d, self.slots["f"])
                c.start()
                self.sent.append(c)
            self.slots["f"] += 1

    def spread(self, n):
        fam, found = self.events(n)
        for s, k, way in found:
            for d in (2, 3, 0, 1):
                self.first_in(s, d).wait_recv()
                c = self.second(s, (d + 2) % 4, self.slots["g"])
                c.start()
                self.sent.append(c)
            self.slots["g"] += 1

    def arrived(self, n):
        fam, found = self.events(n)
        for s, k, way in found:
            for d in range(4):
                self.second_in(s, d).wait_recv()

    def arrived_across(self):
        self.local().wait()
        for d in range(2):
            self.given_on(d).wait_recv()

    def finish(self):
        for c in self.sent:
            c.wait_send()


def greet(at, near):
    barrier = pltpu.get_barrier_semaphore()
    who = [near["across"], near["sibling"], {"yhi": 1 - at["yhi"]}]
    who += [near_z(at, k) for k in range(1, NZ)]
    who += [near_sample(at, k) for k in range(1, 8)]
    for device in who:
        pl.semaphore_signal(barrier, inc=1, device_id=device, device_id_type=MESH_ID)
    pl.semaphore_wait(barrier, len(who))


def near_z(at, k):
    return {"z": lax.rem(at["z"] + k, NZ)}


def near_sample(at, k):
    ylo = at["ylo"] if k < 4 else 1 - at["ylo"]
    return {"ylo": ylo, "x": lax.rem(at["x"] + k % 4, 4)}


GATHER_SEMS = [
    pltpu.SemaphoreType.DMA((17,)),
    pltpu.SemaphoreType.DMA((16,)),
    pltpu.SemaphoreType.DMA((15, 4)),
    pltpu.SemaphoreType.DMA((16, 4)),
    pltpu.SemaphoreType.DMA((14, 4)),
    pltpu.SemaphoreType.DMA((16, 4)),
    pltpu.SemaphoreType.DMA,
]


class Project:
    def __init__(self, at, near, normed, wbuf, part, got, out, sems):
        self.at, self.near, self.normed, self.wbuf = at, near, normed, wbuf
        self.part, self.got, self.out, self.ss, self.rs = part, got, out, *sems

    def dot(self, s):
        w = self.wbuf[s].reshape(2048, 256)
        return jnp.dot(self.normed[...], w, preferred_element_type=jnp.float32).astype(jnp.bfloat16)

    def copy(self, z):
        return pltpu.make_async_remote_copy(
            src_ref=self.part.at[1, z],
            dst_ref=self.got.at[z],
            send_sem=self.ss.at[z],
            recv_sem=self.rs.at[z],
            device_id=self.near["sibling"],
            device_id_type=MESH_ID,
        )

    def columns(self, z):
        c = self.at["head"]
        self.part[1, z] = self.dot((1 - c) * NZ + z)
        self.copy(z).start()
        self.part[0, z] = self.dot(c * NZ + z)

    def combine(self, z):
        self.copy(z).wait_recv()
        total = self.part[0, z].astype(jnp.float32) + self.got[z].astype(jnp.float32)
        start = pl.multiple_of(z * 256, 256)
        self.out[:, pl.ds(start, 256)] = total.astype(jnp.bfloat16)


F32, BF16 = jnp.float32, jnp.bfloat16
NT = (((1,), (1,)), ((), ()))


def mm(a, b):
    return jnp.dot(a, b, preferred_element_type=F32)


def three(v):
    a = v.astype(BF16)
    rest = v - a.astype(F32)
    b = rest.astype(BF16)
    return a, b, (rest - b.astype(F32)).astype(BF16)


def by_column(v, e):
    a, b, c = three(v)
    return mm(a, e) + mm(b, e) + mm(c, e)


def iota(shape, dim):
    return lax.broadcasted_iota(jnp.int32, shape, dim)


def remote(src, dst, send, recv, to):
    return pltpu.make_async_remote_copy(
        src_ref=src,
        dst_ref=dst,
        send_sem=send,
        recv_sem=recv,
        device_id=to,
        device_id_type=MESH_ID,
    )


class Scan:
    def __init__(self, at, sout, sin, dsend, din, init, tsend, eout, entry, sems):
        self.at = at
        self.sout, self.sin, self.dsend, self.din = sout, sin, dsend, din
        self.init, self.tsend, self.eout, self.entry = init, tsend, eout, entry
        self.ss, self.sr, self.ds, self.dr, self.es, self.er, self.ps, self.ir, self.ts = sems

    def peer(self, k):
        return lax.rem(self.at["z"] + k, NZ)

    def state(self, k):
        z, to = self.at["z"], self.peer(k)
        return remote(self.sout.at[to], self.sin.at[z], self.ss.at[k], self.sr.at[z], {"z": to})

    def state_in(self, k):
        z = self.peer(k)
        return remote(self.sout.at[z], self.sin.at[z], self.ss.at[k], self.sr.at[z], {"z": z})

    def decay(self, k):
        z, to = self.at["z"], self.peer(k)
        return remote(self.dsend.at[0], self.din.at[z], self.ds.at[k], self.dr.at[z], {"z": to})

    def decay_in(self, k):
        z = self.peer(k)
        return remote(self.dsend.at[0], self.din.at[z], self.ds.at[k], self.dr.at[z], {"z": z})

    def entering(self, k):
        z, to = self.at["z"], self.peer(k)
        return remote(self.eout.at[to], self.entry.at[z], self.es.at[k], self.er.at[z], {"z": to})

    def entering_in(self, k):
        z = self.peer(k)
        return remote(self.eout.at[z], self.entry.at[z], self.es.at[k], self.er.at[z], {"z": z})

    def prompt(self, k):
        return remote(
            self.tsend, self.init, self.ps.at[k], self.ir, near_sample(self.at, k)
        )

    def total(self):
        return remote(self.tsend, self.init, self.ts, self.ir, {"yhi": 1 - self.at["yhi"]})

    def holds_prompt(self):
        m = self.at["ylo"] * 4 + self.at["x"]
        return (m == self.at["z"]) & (self.at["yhi"] == 0)

    def send_prompt(self, prompt_hbm, prompt_vmem, sem):
        @pl.when(self.holds_prompt())
        def _():
            load = pltpu.make_async_copy(prompt_hbm, prompt_vmem, sem)
            load.start()
            load.wait()
            eye = (iota((16, 16), 0) == iota((16, 16), 1)).astype(F32).astype(BF16)
            low = prompt_vmem[...].astype(BF16)
            turned = lax.dot_general(eye, low, NT, preferred_element_type=F32).astype(BF16)
            self.tsend[...] = turned
            self.init[...] = turned
            for k in range(1, 8):
                self.prompt(k).start()

    def send_states(self):
        for k in range(1, NZ):
            self.state(k).start()
            self.decay(k).start()
        z = self.at["z"]
        self.sin[z] = self.sout[z]
        self.din[z] = self.dsend[0]

    def combine(self, hi):
        @pl.when(self.at["yhi"] == hi)
        def _():
            for k in range(1, NZ):
                self.state_in(k).wait_recv()
                self.decay_in(k).wait_recv()
            if hi == 0:
                @pl.when(self.holds_prompt())
                def _():
                    for k in range(1, 8):
                        self.prompt(k).wait_send()

                @pl.when(jnp.logical_not(self.holds_prompt()))
                def _():
                    self.prompt(1).wait_recv()
            else:
                self.total().wait_recv()

            def step(j, acc):
                self.eout[j] = acc.astype(BF16)
                return acc * self.din[j] + self.sin[j].astype(F32)

            acc = lax.fori_loop(0, NZ, step, self.init[...].astype(F32))
            if hi == 0:
                self.tsend[...] = acc.astype(BF16)
                self.total().start()
            for k in range(1, NZ):
                self.entering(k).start()
            z = self.at["z"]
            self.entry[z] = self.eout[z]

    def entered(self):
        for k in range(1, NZ):
            self.entering_in(k).wait_recv()

    def finish(self):
        for k in range(1, NZ):
            self.state(k).wait_send()
            self.decay(k).wait_send()
            self.entering(k).wait_send()

        @pl.when(self.at["yhi"] == 0)
        def _():
            self.total().wait_send()


SCAN_SEMS = [pltpu.SemaphoreType.DMA((NZ,))] * 7 + [pltpu.SemaphoreType.DMA] * 2


class Local:
    def __init__(self, **refs):
        self.__dict__.update(refs)

    def prepare(self):
        self.e[...] = (iota((32, 2048), 0) == lax.shift_right_logical(iota((32, 2048), 1), 6)).astype(F32).astype(BF16)
        tri = (iota((L, L), 0) >= iota((L, L), 1)).astype(F32).astype(BF16)
        eye = (iota((32, 32), 0) == iota((32, 32), 1)).astype(F32).astype(BF16)
        self.bt[...] = self.b_in[...].astype(F32).T.astype(BF16)
        for b in range(2):
            rows = slice(b * L, b * L + L)
            parts = three(self.log_decay[rows])
            run = sum(mm(tri, part) for part in parts)
            self.run[rows] = run
            turned = [lax.dot_general(eye, part, NT, preferred_element_type=F32) for part in three(run)]
            self.runt[b] = turned[0] + turned[1] + turned[2]
            self.scores[b] = mm(self.c_out[rows], self.bt[:, rows])
        ends = [self.run[L - 1 : L], self.run[2 * L - 1 : 2 * L]]
        line = iota((8, 32), 0)
        self.lines[...] = jnp.where(
            line == 0,
            jnp.exp(ends[0]),
            jnp.where(
                line == 1,
                jnp.exp(ends[1]),
                jnp.where(line == 2, jnp.exp(ends[0] + ends[1]), self.skip_gain[...]),
            ),
        )

    def states(self, lo, hi):
        def group(g, _):
            cols = pl.ds(pl.multiple_of(g * 512, 512), 512)
            e = self.e[:, cols]
            wide = by_column(self.lines[...], e)
            self.wide[:, cols] = wide
            self.dsend[0, :, cols] = wide[2:3]
            found = []
            for b in range(2):
                rows = slice(b * L, b * L + L)
                run = self.run[rows]
                self.re[rows, cols] = by_column(run, e)
                scaled = (self.values[rows, cols].astype(F32) * by_column(self.step[rows], e)).astype(BF16)
                self.scaled[rows, cols] = scaled
                tail = by_column(jnp.exp(run[L - 1 : L] - run), e)
                weighted = (scaled.astype(F32) * tail).astype(BF16)
                found.append(mm(self.bt[:, rows], weighted))
            self.bs0[:, cols] = found[0]
            state = (wide[1:2] * found[0] + found[1]).astype(BF16)
            self.sout[:, :, cols] = state.reshape(NZ, 16, 512)
            return 0

        lax.fori_loop(lo, hi, group, 0)

    def mix(self, b, lo, hi):
        half = L // 2
        keep = iota((half, half), 0) >= iota((half, half), 1)
        first = iota((L, 128), 1) < P_SIZE
        rows = slice(b * L, b * L + L)

        def pair(j, _):
            cols = pl.ds(pl.multiple_of(j * 128, 128), 128)
            scaled = self.scaled[rows, cols]
            re = self.re[rows, cols]
            made = []
            for one in range(2):
                col = re[:, one * P_SIZE : one * P_SIZE + 1]
                row = self.runt[b, pl.ds(2 * j + one, 1), :]
                top = jnp.exp(jnp.where(keep, col[:half] - row[:, :half], -1e30))
                top = (self.scores[b, :half, :half] * top).astype(BF16)
                left = jnp.exp(col[half:] - row[:, :half])
                left = (self.scores[b, half:, :half] * left).astype(BF16)
                right = jnp.exp(jnp.where(keep, col[half:] - row[:, half:], -1e30))
                right = (self.scores[b, half:, half:] * right).astype(BF16)
                under = mm(jnp.concatenate([left, right], axis=1), scaled)
                made.append(jnp.concatenate([mm(top, scaled[:half]), under], axis=0))
            self.lout[rows, cols] = jnp.where(first, made[0], made[1])
            return 0

        lax.fori_loop(lo, hi, pair, 0)

    def normalize(self, b, lo, hi):
        def group(g, _):
            cols = pl.ds(pl.multiple_of(g * 512, 512), 512)
            start = self.entry[:, :, cols].reshape(128, 512)
            if b == 1:
                start = (self.wide[0:1, cols] * start.astype(F32) + self.bs0[:, cols]).astype(BF16)
            for r in range(b * L, b * L + L, 128):
                rows = slice(r, r + 128)
                carried = jnp.exp(self.re[rows, cols]) * mm(self.c_out[rows], start)
                out = self.lout[rows, cols] + self.wide[3:4, cols] * self.values[rows, cols].astype(F32)
                out = out + carried
                v = self.gate[rows, cols].astype(F32)
                gated = out * (0.5 * v * (1.0 + jnp.tanh(0.5 * v)))
                mean = jnp.sum(gated * gated, axis=1, keepdims=True) * (1.0 / 512)
                scaled = gated * lax.rsqrt(mean + EPSILON) * self.norm_gain[:, cols]
                self.normed[rows, cols] = scaled.astype(BF16)
            return 0

        lax.fori_loop(lo, hi, group, 0)


def kernel(
    own, values_hbm, gate_hbm, prompt_hbm, b_in, c_out, step, log_decay, skip_gain, norm_gain,
    result,
    wbuf, part, got, values, gate, scaled, re, lout, normed, bs0, scores, run, runt, e, bt,
    lines, wide, sout, sin, dsend, din, init, tsend, eout, entry, prompt, load, *sems,
):
    at, near = place()
    first = pltpu.make_async_copy(values_hbm, values, load.at[0])
    second = pltpu.make_async_copy(gate_hbm, gate, load.at[1])
    first.start()
    second.start()
    greet(at, near)
    gather = Gather(at, near, own, wbuf, sems[:7])
    scan = Scan(at, sout, sin, dsend, din, init, tsend, eout, entry, sems[7:16])
    proj = Project(at, near, normed, wbuf, part, got, result, sems[16:18])
    local = Local(
        b_in=b_in, c_out=c_out, step=step, log_decay=log_decay, skip_gain=skip_gain, norm_gain=norm_gain,
        values=values, gate=gate, scaled=scaled, re=re, lout=lout, normed=normed, bs0=bs0, scores=scores,
        run=run, runt=runt, e=e, bt=bt, lines=lines, wide=wide, sout=sout, dsend=dsend, entry=entry,
    )
    z = at["z"]

    def columns(k):
        proj.columns(lax.rem(z + k, NZ))
        if 0 < k < 4:
            proj.columns(lax.rem(z + NZ - k, NZ))

    def combine(k):
        proj.combine(lax.rem(z + k, NZ))
        if 0 < k < 4:
            proj.combine(lax.rem(z + NZ - k, NZ))

    gather.begin()
    scan.send_prompt(prompt_hbm, prompt, load.at[2])
    local.prepare()
    first.wait()
    local.states(0, 2)
    gather.forward(0)
    local.states(2, 4)
    scan.send_states()
    gather.begin_across()
    local.mix(0, 0, 8)
    gather.forward(1)
    gather.spread(0)
    local.mix(0, 8, 16)
    scan.combine(0)
    gather.forward(2)
    gather.spread(1)
    local.mix(1, 0, 8)
    scan.combine(1)
    gather.forward(3)
    gather.spread(2)
    local.mix(1, 8, 16)
    second.wait()
    scan.entered()
    local.normalize(0, 0, 4)
    gather.forward(4)
    gather.spread(3)
    local.normalize(1, 0, 4)
    gather.arrived_across()
    columns(0)
    gather.arrived(0)
    gather.arrived(1)
    columns(1)
    gather.forward(5)
    gather.spread(4)
    combine(0)
    combine(1)
    gather.arrived(2)
    gather.arrived(3)
    columns(2)
    gather.forward(6)
    gather.spread(5)
    combine(2)
    gather.forward(7)
    gather.spread(6)
    gather.arrived(4)
    gather.arrived(5)
    columns(3)
    gather.spread(7)
    combine(3)
    gather.arrived(6)
    gather.arrived(7)
    columns(4)
    combine(4)
    for k in range(NZ):
        proj.copy(k).wait_send()
    scan.finish()
    gather.finish()


def shards(
    values,
    gate_values,
    state_in,
    state_out,
    step_size,
    log_decay,
    skip_gain,
    norm_gain,
    out_weight,
    prompt_state,
):
    vmem = pl.BlockSpec(memory_space=pltpu.VMEM)
    hbm = pl.BlockSpec(memory_space=pl.ANY)
    out = pl.pallas_call(
        kernel,
        name="layer",
        out_shape=jax.ShapeDtypeStruct((512, 2048), BF16),
        in_specs=[hbm] * 4 + [vmem] * 6,
        out_specs=vmem,
        scratch_shapes=[
            pltpu.VMEM((16, 16, 128, 256), BF16),
            pltpu.VMEM((2, NZ, 512, 256), BF16),
            pltpu.VMEM((NZ, 512, 256), BF16),
            pltpu.VMEM((512, 2048), BF16),
            pltpu.VMEM((512, 2048), BF16),
            pltpu.VMEM((512, 2048), BF16),
            pltpu.VMEM((512, 2048), F32),
            pltpu.VMEM((512, 2048), F32),
            pltpu.VMEM((512, 2048), BF16),
            pltpu.VMEM((128, 2048), F32),
            pltpu.VMEM((2, L, L), F32),
            pltpu.VMEM((512, 32), F32),
            pltpu.VMEM((2, 32, L), F32),
            pltpu.VMEM((32, 2048), BF16),
            pltpu.VMEM((128, 512), BF16),
            pltpu.VMEM((8, 32), F32),
            pltpu.VMEM((8, 2048), F32),
            pltpu.VMEM((NZ, 16, 2048), BF16),
            pltpu.VMEM((NZ, 16, 2048), BF16),
            pltpu.VMEM((1, 1, 2048), F32),
            pltpu.VMEM((NZ, 1, 2048), F32),
            pltpu.VMEM((16, 2048), BF16),
            pltpu.VMEM((16, 2048), BF16),
            pltpu.VMEM((NZ, 16, 2048), BF16),
            pltpu.VMEM((NZ, 16, 2048), BF16),
            pltpu.VMEM((2048, 16), F32),
            pltpu.SemaphoreType.DMA((3,)),
            *GATHER_SEMS,
            *SCAN_SEMS,
            pltpu.SemaphoreType.DMA((NZ,)),
            pltpu.SemaphoreType.DMA((NZ,)),
        ],
        compiler_params=pltpu.CompilerParams(
            collective_id=0, has_side_effects=True, vmem_limit_bytes=56 << 20
        ),
    )(
        out_weight.reshape(16, 128, 256),
        values[0],
        gate_values[0],
        prompt_state.reshape(2048, 16),
        state_in[0],
        state_out[0],
        step_size[0],
        log_decay[0],
        skip_gain.reshape(1, 32),
        norm_gain.reshape(1, 2048),
    )
    return out[None]


def solution(mesh):
    split = Mesh(mesh.devices.reshape(2, 4, 2, NZ, 2), ("ylo", "x", "yhi", "z", "head"))
    return jax.shard_map(
        shards,
        mesh=split,
        in_specs=(
            P(SAMPLE, SEQ, "head"),
            P(SAMPLE, SEQ, "head"),
            P(SAMPLE, SEQ, None),
            P(SAMPLE, SEQ, None),
            P(SAMPLE, SEQ, "head"),
            P(SAMPLE, SEQ, "head"),
            P("head"),
            P("head"),
            P("head", SEQ),
            P("head", None, SAMPLE),
        ),
        out_specs=P(SAMPLE, SEQ, "head"),
        check_vma=False,
    )
```

```python
from functools import partial

import jax
import jax.numpy as jnp
from jax import lax
from jax.experimental import pallas as pl
from jax.experimental.pallas import tpu as pltpu
from jax.sharding import Mesh
from jax.sharding import PartitionSpec as P

P_SIZE = 64
L = 256
GROUP_HEADS = 8
SEQ = ("yhi", "z")
SAMPLE = ("ylo", "x")
NZ = 8
MESH_ID = pl.DeviceIdType.MESH
EPSILON = 1e-05


def place():
    names = ("ylo", "x", "yhi", "z", "head")
    at = {name: lax.axis_index(name) for name in names}
    y = at["yhi"] * 2 + at["ylo"]
    up, down = lax.rem(y + 1, 4), lax.rem(y + 3, 4)
    near = {
        "+x": {"x": lax.rem(at["x"] + 1, 4)},
        "-x": {"x": lax.rem(at["x"] + 3, 4)},
        "+y": {"yhi": up // 2, "ylo": lax.rem(up, 2)},
        "-y": {"yhi": down // 2, "ylo": lax.rem(down, 2)},
        "+z": {"z": lax.rem(at["z"] + 1, NZ)},
        "-z": {"z": lax.rem(at["z"] + NZ - 1, NZ)},
        "across": {"yhi": 1 - at["yhi"], "ylo": 1 - at["ylo"]},
        "beside": {"ylo": 1 - at["ylo"]},
        "sibling": {"head": 1 - at["head"]},
    }
    return at, near


WAYS = ("+x", "-x", "+y", "-y")


class Gather:
    def __init__(self, at, near, own, wbuf, sems):
        self.at, self.near, self.own, self.wbuf = at, near, own, wbuf
        self.zs, self.zr, self.fs, self.fr, self.gs, self.gr, self.ls = sems
        px, lo = lax.rem(at["x"], 2), at["ylo"]
        self.mine = px * 2 + lo
        self.byx = (1 - px) * 2 + lo
        self.byy = px * 2 + 1 - lo
        self.px = px
        self.s_own = at["yhi"] * NZ + at["z"]
        self.s_across = (1 - at["yhi"]) * NZ + at["z"]

    def copy(self, src, s, start, size, send, recv, to):
        dst = self.wbuf.at[s, pl.ds(start, size)]
        return pltpu.make_async_remote_copy(
            src_ref=dst if src is None else src,
            dst_ref=dst,
            send_sem=send,
            recv_sem=recv,
            device_id=self.near[to],
            device_id_type=MESH_ID,
        )

    def shard(self, fam, z):
        hi = self.at["yhi"] if fam == 0 else 1 - self.at["yhi"]
        return hi * NZ + lax.rem(z + 2 * NZ, NZ)

    def events(self, n):
        fam, k = n % 2, n // 2
        found = []
        if k < (4 if fam == 0 else 3):
            found.append((self.shard(fam, self.at["z"] - 1 - k), k, "+z"))
        if k < (3 if fam == 0 else 4):
            found.append((self.shard(fam, self.at["z"] + 1 + k), k, "-z"))
        return fam, found

    def ring(self, s, way, slot, src=None):
        return self.copy(src, s, self.mine * 4, 4, self.zs.at[slot], self.zr.at[s], way)

    def local(self):
        return pltpu.make_async_copy(self.own, self.wbuf.at[self.s_own], self.ls)

    def give(self):
        src = self.own.at[pl.ds(self.byy * 4, 4)]
        to = self.zr.at[self.s_own]
        return self.copy(src, self.s_own, self.byy * 4, 4, self.zs.at[0], to, "across")

    def given(self):
        to = self.zr.at[self.s_across]
        return self.copy(None, self.s_across, self.mine * 4, 4, self.zs.at[0], to, "across")

    def lend(self):
        to = self.fr.at[self.s_across, 2]
        return self.copy(None, self.s_across, self.mine * 4, 4, self.zs.at[15], to, "beside")

    def lent(self):
        to = self.fr.at[self.s_across, 2]
        return self.copy(None, self.s_across, self.byy * 4, 4, self.zs.at[15], to, "beside")

    def give_on(self, d):
        start = (self.mine if d == 0 else self.byy) * 4
        return self.copy(
            None, self.s_across, start, 4, self.fs.at[0, d], self.fr.at[self.s_across, d], WAYS[d]
        )

    def given_on(self, d):
        start = (self.byx if d == 0 else 3 - self.mine) * 4
        return self.copy(
            None, self.s_across, start, 4, self.fs.at[0, d], self.fr.at[self.s_across, d], WAYS[d]
        )

    def first(self, s, d, slot):
        start = self.mine * 4 + 2 * (d % 2)
        return self.copy(None, s, start, 2, self.fs.at[slot, d], self.fr.at[s, d], WAYS[d])

    def first_in(self, s, d):
        start = (self.byx if d < 2 else self.byy) * 4 + 2 * (d % 2)
        return self.copy(None, s, start, 2, self.fs.at[0, d], self.fr.at[s, d], WAYS[d])

    def second(self, s, d, slot):
        start = (self.byy if d < 2 else self.byx) * 4 + (0, 2, 1, 3)[d]
        return self.copy(None, s, start, 1, self.gs.at[slot, d], self.gr.at[s, d], WAYS[d])

    def second_in(self, s, d):
        far = 3 - self.mine
        start = far * 4 + (0, 2, 1, 3)[d]
        return self.copy(None, s, start, 1, self.gs.at[0, d], self.gr.at[s, d], WAYS[d])

    def begin(self):
        src = self.own.at[pl.ds(self.mine * 4, 4)]
        self.sent = []
        for c in (
            self.ring(self.s_own, "+z", 1, src),
            self.ring(self.s_own, "-z", 2, src),
            self.give(),
        ):
            c.start()
            self.sent.append(c)
        self.local().start()
        self.slots = {"z": 5, "f": 1, "g": 0}

    def begin_across(self):
        self.given().wait_recv()
        for c in (
            self.ring(self.s_across, "+z", 3),
            self.ring(self.s_across, "-z", 4),
            self.give_on(0),
            self.lend(),
        ):
            c.start()
            self.sent.append(c)

    def go_on_across(self):
        self.lent().wait_recv()
        c = self.give_on(1)
        c.start()
        self.sent.append(c)

    def forward(self, n):
        fam, found = self.events(n)
        for s, k, way in found:
            self.ring(s, way, 0).wait_recv()
            last = k + 1 == ((4 if fam == 0 else 3) if way == "+z" else (3 if fam == 0 else 4))
            if not last:
                c = self.ring(s, way, self.slots["z"])
                self.slots["z"] += 1
                c.start()
                self.sent.append(c)
            for d in range(4):
                c = self.first(s, d, self.slots["f"])
                c.start()
                self.sent.append(c)
            self.slots["f"] += 1

    def spread(self, n):
        fam, found = self.events(n)
        for s, k, way in found:
            for d in (2, 3, 0, 1):
                self.first_in(s, d).wait_recv()
                c = self.second(s, (d + 2) % 4, self.slots["g"])
                c.start()
                self.sent.append(c)
            self.slots["g"] += 1

    def arrived(self, n):
        fam, found = self.events(n)
        for s, k, way in found:
            for d in range(4):
                self.second_in(s, d).wait_recv()

    def arrived_across(self):
        self.local().wait()
        for d in range(2):
            self.given_on(d).wait_recv()

    def finish(self):
        for c in self.sent:
            c.wait_send()


def greet(at, near):
    barrier = pltpu.get_barrier_semaphore()
    who = [near["across"], near["sibling"], {"yhi": 1 - at["yhi"]}]
    who += [near_z(at, k) for k in range(1, NZ)]
    who += [near_sample(at, k) for k in range(1, 8)]
    for device in who:
        pl.semaphore_signal(barrier, inc=1, device_id=device, device_id_type=MESH_ID)
    pl.semaphore_wait(barrier, len(who))


def near_z(at, k):
    return {"z": lax.rem(at["z"] + k, NZ)}


def near_sample(at, k):
    ylo = at["ylo"] if k < 4 else 1 - at["ylo"]
    return {"ylo": ylo, "x": lax.rem(at["x"] + k % 4, 4)}


GATHER_SEMS = [
    pltpu.SemaphoreType.DMA((17,)),
    pltpu.SemaphoreType.DMA((16,)),
    pltpu.SemaphoreType.DMA((15, 4)),
    pltpu.SemaphoreType.DMA((16, 4)),
    pltpu.SemaphoreType.DMA((14, 4)),
    pltpu.SemaphoreType.DMA((16, 4)),
    pltpu.SemaphoreType.DMA,
]


class Project:
    def __init__(self, at, near, normed, wbuf, part, got, out, sems):
        self.at, self.near, self.normed, self.wbuf = at, near, normed, wbuf
        self.part, self.got, self.out, self.ss, self.rs = part, got, out, *sems

    def dot(self, s):
        w = self.wbuf[s].reshape(2048, 256)
        return jnp.dot(self.normed[...], w, preferred_element_type=jnp.float32).astype(jnp.bfloat16)

    def copy(self, z):
        return pltpu.make_async_remote_copy(
            src_ref=self.part.at[1, z],
            dst_ref=self.got.at[z],
            send_sem=self.ss.at[z],
            recv_sem=self.rs.at[z],
            device_id=self.near["sibling"],
            device_id_type=MESH_ID,
        )

    def columns(self, z):
        c = self.at["head"]
        self.part[1, z] = self.dot((1 - c) * NZ + z)
        self.copy(z).start()
        self.part[0, z] = self.dot(c * NZ + z)

    def combine(self, z):
        self.copy(z).wait_recv()
        total = self.part[0, z].astype(jnp.float32) + self.got[z].astype(jnp.float32)
        start = pl.multiple_of(z * 256, 256)
        self.out[:, pl.ds(start, 256)] = total.astype(jnp.bfloat16)


F32, BF16 = jnp.float32, jnp.bfloat16


def mm(a, b):
    return jnp.dot(a, b, preferred_element_type=F32)


def nt(a, b):
    return lax.dot_general(a, b, (((1,), (1,)), ((), ())), preferred_element_type=F32)


def three(v):
    a = v.astype(BF16)
    rest = v - a.astype(F32)
    b = rest.astype(BF16)
    return a, b, (rest - b.astype(F32)).astype(BF16)


def by_column(v, e):
    a, b, c = three(v)
    return mm(a, e) + mm(b, e) + mm(c, e)


def iota(shape, dim):
    return lax.broadcasted_iota(jnp.int32, shape, dim)


def remote(src, dst, send, recv, to):
    return pltpu.make_async_remote_copy(
        src_ref=src,
        dst_ref=dst,
        send_sem=send,
        recv_sem=recv,
        device_id=to,
        device_id_type=MESH_ID,
    )


class Scan:
    def __init__(self, at, sout, sin, dsend, din, init, tsend, eout, entry, sems):
        self.at = at
        self.sout, self.sin, self.dsend, self.din = sout, sin, dsend, din
        self.init, self.tsend, self.eout, self.entry = init, tsend, eout, entry
        self.ss, self.sr, self.ds, self.dr, self.es, self.er, self.ps, self.ir, self.ts = sems

    def peer(self, k):
        return lax.rem(self.at["z"] + k, NZ)

    def state(self, k):
        z, to = self.at["z"], self.peer(k)
        return remote(self.sout.at[to], self.sin.at[z], self.ss.at[k], self.sr.at[z], {"z": to})

    def state_in(self, k):
        z = self.peer(k)
        return remote(self.sout.at[z], self.sin.at[z], self.ss.at[k], self.sr.at[z], {"z": z})

    def decay(self, k):
        z, to = self.at["z"], self.peer(k)
        return remote(self.dsend.at[0], self.din.at[z], self.ds.at[k], self.dr.at[z], {"z": to})

    def decay_in(self, k):
        z = self.peer(k)
        return remote(self.dsend.at[0], self.din.at[z], self.ds.at[k], self.dr.at[z], {"z": z})

    def entering(self, k):
        z, to = self.at["z"], self.peer(k)
        return remote(self.eout.at[to], self.entry.at[z], self.es.at[k], self.er.at[z], {"z": to})

    def entering_in(self, k):
        z = self.peer(k)
        return remote(self.eout.at[z], self.entry.at[z], self.es.at[k], self.er.at[z], {"z": z})

    def prompt(self, k):
        return remote(
            self.tsend, self.init, self.ps.at[k], self.ir, near_sample(self.at, k)
        )

    def total(self):
        return remote(self.tsend, self.init, self.ts, self.ir, {"yhi": 1 - self.at["yhi"]})

    def holds_prompt(self):
        m = self.at["ylo"] * 4 + self.at["x"]
        return (m == self.at["z"]) & (self.at["yhi"] == 0)

    def send_prompt(self, prompt_hbm, prompt_vmem, sem):
        @pl.when(self.holds_prompt())
        def _():
            load = pltpu.make_async_copy(prompt_hbm, prompt_vmem, sem)
            load.start()
            load.wait()
            for j in range(0, 32, 2):
                two = jnp.concatenate([prompt_vmem[j], prompt_vmem[j + 1]], axis=1).astype(BF16)
                self.tsend[:, j * P_SIZE : (j + 2) * P_SIZE] = two
                self.init[:, j * P_SIZE : (j + 2) * P_SIZE] = two
            for k in range(1, 8):
                self.prompt(k).start()

    def send_states(self):
        for k in range(1, NZ):
            self.state(k).start()
            self.decay(k).start()
        z = self.at["z"]
        self.sin[z] = self.sout[z]
        self.din[z] = self.dsend[0]

    def combine(self, hi):
        @pl.when(self.at["yhi"] == hi)
        def _():
            for k in range(1, NZ):
                self.state_in(k).wait_recv()
                self.decay_in(k).wait_recv()
            if hi == 0:
                @pl.when(self.holds_prompt())
                def _():
                    for k in range(1, 8):
                        self.prompt(k).wait_send()

                @pl.when(jnp.logical_not(self.holds_prompt()))
                def _():
                    self.prompt(1).wait_recv()
            else:
                self.total().wait_recv()

            def step(j, acc):
                self.eout[j] = acc.astype(BF16)
                return acc * self.din[j] + self.sin[j].astype(F32)

            acc = lax.fori_loop(0, NZ, step, self.init[...].astype(F32))
            if hi == 0:
                self.tsend[...] = acc.astype(BF16)
                self.total().start()
            for k in range(1, NZ):
                self.entering(k).start()
            z = self.at["z"]
            self.entry[z] = self.eout[z]

    def entered(self):
        for k in range(1, NZ):
            self.entering_in(k).wait_recv()

    def finish(self):
        for k in range(1, NZ):
            self.state(k).wait_send()
            self.decay(k).wait_send()
            self.entering(k).wait_send()

        @pl.when(self.at["yhi"] == 0)
        def _():
            self.total().wait_send()


SCAN_SEMS = [pltpu.SemaphoreType.DMA((NZ,))] * 7 + [pltpu.SemaphoreType.DMA] * 2


class Local:
    def __init__(self, **refs):
        self.__dict__.update(refs)

    def prepare(self):
        self.e[...] = (iota((32, 2048), 0) == lax.shift_right_logical(iota((32, 2048), 1), 6)).astype(F32).astype(BF16)
        tri = (iota((L, L), 0) >= iota((L, L), 1)).astype(F32).astype(BF16)
        eye = (iota((L, L), 0) == iota((L, L), 1)).astype(F32).astype(BF16)
        small = (iota((32, 32), 0) == iota((32, 32), 1)).astype(F32).astype(BF16)
        self.bt[...] = self.b_in[...].astype(F32).T.astype(BF16)
        for b in range(2):
            rows = slice(b * L, b * L + L)
            a, m, c = [nt(tri, part) for part in three(self.log_decay[:, rows])]
            run = a + m + c
            self.run[rows] = run
            a, m, c = [nt(small, part) for part in three(run)]
            self.runt[b] = a + m + c
            a, m, c = [nt(eye, part) for part in three(self.step[:, rows])]
            self.stept[rows] = a + m + c
            self.scores[b] = mm(self.c_out[rows], self.bt[:, rows])
        ends = [self.run[L - 1 : L], self.run[2 * L - 1 : 2 * L]]
        line = iota((8, 32), 0)
        self.lines[...] = jnp.where(
            line == 0,
            jnp.exp(ends[0]),
            jnp.where(
                line == 1,
                jnp.exp(ends[1]),
                jnp.where(line == 2, jnp.exp(ends[0] + ends[1]), self.skip_gain[...]),
            ),
        )

    def states(self, lo, hi):
        def group(g, _):
            cols = pl.ds(pl.multiple_of(g * 512, 512), 512)
            e = self.e[:, cols]
            wide = by_column(self.lines[...], e)
            self.wide[:, cols] = wide
            self.dsend[0, :, cols] = wide[2:3]
            found = []
            for b in range(2):
                rows = slice(b * L, b * L + L)
                run = self.run[rows]
                self.re[rows, cols] = by_column(run, e)
                scaled = (self.values[rows, cols].astype(F32) * by_column(self.stept[rows], e)).astype(BF16)
                self.scaled[rows, cols] = scaled
                tail = by_column(jnp.exp(run[L - 1 : L] - run), e)
                weighted = (scaled.astype(F32) * tail).astype(BF16)
                found.append(mm(self.bt[:, rows], weighted))
            self.bs0[:, cols] = found[0]
            state = (wide[1:2] * found[0] + found[1]).astype(BF16)
            self.sout[:, :, cols] = state.reshape(NZ, 16, 512)
            return 0

        lax.fori_loop(lo, hi, group, 0)

    def mix(self, b, lo, hi):
        half = L // 2
        keep = iota((half, half), 0) >= iota((half, half), 1)
        first = iota((L, 128), 1) < P_SIZE
        rows = slice(b * L, b * L + L)

        def pair(j, _):
            cols = pl.ds(pl.multiple_of(j * 128, 128), 128)
            scaled = self.scaled[rows, cols]
            re = self.re[rows, cols]
            made = []
            for one in range(2):
                col = re[:, one * P_SIZE : one * P_SIZE + 1]
                row = self.runt[b, pl.ds(2 * j + one, 1), :]
                top = jnp.exp(jnp.where(keep, col[:half] - row[:, :half], -1e30))
                top = (self.scores[b, :half, :half] * top).astype(BF16)
                left = jnp.exp(col[half:] - row[:, :half])
                left = (self.scores[b, half:, :half] * left).astype(BF16)
                right = jnp.exp(jnp.where(keep, col[half:] - row[:, half:], -1e30))
                right = (self.scores[b, half:, half:] * right).astype(BF16)
                under = mm(jnp.concatenate([left, right], axis=1), scaled)
                made.append(jnp.concatenate([mm(top, scaled[:half]), under], axis=0))
            self.lout[rows, cols] = jnp.where(first, made[0], made[1])
            return 0

        lax.fori_loop(lo, hi, pair, 0)

    def normalize(self, b, lo, hi):
        def group(g, _):
            cols = pl.ds(pl.multiple_of(g * 512, 512), 512)
            start = self.entry[:, :, cols].reshape(128, 512)
            if b == 1:
                start = (self.wide[0:1, cols] * start.astype(F32) + self.bs0[:, cols]).astype(BF16)
            for r in range(b * L, b * L + L, 128):
                rows = slice(r, r + 128)
                carried = jnp.exp(self.re[rows, cols]) * mm(self.c_out[rows], start)
                out = self.lout[rows, cols] + self.wide[3:4, cols] * self.values[rows, cols].astype(F32)
                out = out + carried
                v = self.gate[rows, cols].astype(F32)
                gated = out * (0.5 * v * (1.0 + jnp.tanh(0.5 * v)))
                mean = jnp.sum(gated * gated, axis=1, keepdims=True) * (1.0 / 512)
                scaled = gated * lax.rsqrt(mean + EPSILON) * self.norm_gain[:, cols]
                self.normed[rows, cols] = scaled.astype(BF16)
            return 0

        lax.fori_loop(lo, hi, group, 0)


ORDER = (
    ("s", 0, 2), ("z", 0), ("across",), ("s", 2, 4), ("send",), ("m", 0, 0, 8), ("across2",), ("m", 0, 8, 16),
    ("z", 1), ("z", 2), ("m", 1, 0, 8), ("x", 0), ("x", 1), ("m", 1, 8, 16), ("z", 3), ("z", 4), ("scan", 0),
    ("z", 5), ("z", 6), ("x", 2), ("x", 3), ("scan", 1), ("z", 7), ("gate",), ("entered",), ("n", 0, 0, 4),
    ("n", 1, 0, 4), ("x", 4), ("x", 5), ("across3",), ("c", 0), ("r", 0), ("r", 1), ("c", 1), ("x", 6), ("x", 7),
    ("r", 2), ("r", 3), ("c", 2), ("o", 0), ("o", 1), ("r", 4), ("r", 5), ("c", 3), ("o", 2), ("o", 3), ("r", 6),
    ("r", 7), ("c", 4), ("o", 4),
)


def kernel(
    own, values_hbm, gate_hbm, prompt_hbm, b_hbm, c_hbm, step_hbm, decay_hbm, skip_hbm, norm_hbm,
    result, b_in, c_out, step, log_decay, skip_gain, norm_gain,
    wbuf, part, got, values, gate, scaled, re, lout, bs0, scores, run, runt, stept, e, bt,
    lines, wide, sout, sin, dsend, din, init, tsend, eout, entry, prompt, load, *sems,
):
    at, near = place()
    normed = scaled
    pairs = (
        (decay_hbm, log_decay), (step_hbm, step), (b_hbm, b_in), (c_hbm, c_out), (skip_hbm, skip_gain),
        (values_hbm, values), (norm_hbm, norm_gain), (gate_hbm, gate),
    )
    loads = [pltpu.make_async_copy(src, dst, load.at[i]) for i, (src, dst) in enumerate(pairs)]
    for copy in loads:
        copy.start()
    greet(at, near)
    gather = Gather(at, near, own, wbuf, sems[:7])
    scan = Scan(at, sout, sin, dsend, din, init, tsend, eout, entry, sems[7:16])
    proj = Project(at, near, normed, wbuf, part, got, result, sems[16:18])
    local = Local(
        b_in=b_in, c_out=c_out, step=step, log_decay=log_decay, skip_gain=skip_gain, norm_gain=norm_gain,
        values=values, gate=gate, scaled=scaled, re=re, lout=lout, normed=normed, bs0=bs0, scores=scores,
        run=run, runt=runt, stept=stept, e=e, bt=bt, lines=lines, wide=wide, sout=sout, dsend=dsend, entry=entry,
    )
    z = at["z"]

    def columns(k):
        proj.columns(lax.rem(z + k, NZ))
        if 0 < k < 4:
            proj.columns(lax.rem(z + NZ - k, NZ))

    def combine(k):
        proj.combine(lax.rem(z + k, NZ))
        if 0 < k < 4:
            proj.combine(lax.rem(z + NZ - k, NZ))

    steps = {
        "z": gather.forward,
        "x": gather.spread,
        "r": gather.arrived,
        "s": local.states,
        "m": local.mix,
        "n": local.normalize,
        "c": columns,
        "o": combine,
        "across": gather.begin_across,
        "across2": gather.go_on_across,
        "across3": gather.arrived_across,
        "scan": scan.combine,
        "send": scan.send_states,
        "entered": scan.entered,
        "gate": lambda: (loads[6].wait(), loads[7].wait()),
    }
    gather.begin()
    scan.send_prompt(prompt_hbm, prompt, load.at[8])
    for copy in loads[:5]:
        copy.wait()
    local.prepare()
    loads[5].wait()
    for what, *how in ORDER:
        steps[what](*how)
    for k in range(NZ):
        proj.copy(k).wait_send()
    scan.finish()
    gather.finish()


def shards(
    values,
    gate_values,
    state_in,
    state_out,
    step_size,
    log_decay,
    skip_gain,
    norm_gain,
    out_weight,
    prompt_state,
):
    vmem = pl.BlockSpec(memory_space=pltpu.VMEM)
    hbm = pl.BlockSpec(memory_space=pltpu.HBM)
    out = pl.pallas_call(
        kernel,
        name="layer",
        out_shape=jax.ShapeDtypeStruct((512, 2048), BF16),
        in_specs=[hbm] * 10,
        out_specs=vmem,
        scratch_shapes=[
            pltpu.VMEM((512, 128), BF16),
            pltpu.VMEM((512, 128), BF16),
            pltpu.VMEM((32, 512), F32),
            pltpu.VMEM((32, 512), F32),
            pltpu.VMEM((1, 32), F32),
            pltpu.VMEM((1, 2048), F32),
            pltpu.VMEM((16, 16, 128, 256), BF16),
            pltpu.VMEM((2, NZ, 512, 256), BF16),
            pltpu.VMEM((NZ, 512, 256), BF16),
            pltpu.VMEM((512, 2048), BF16),
            pltpu.VMEM((512, 2048), BF16),
            pltpu.VMEM((512, 2048), BF16),
            pltpu.VMEM((512, 2048), F32),
            pltpu.VMEM((512, 2048), F32),
            pltpu.VMEM((128, 2048), F32),
            pltpu.VMEM((2, L, L), F32),
            pltpu.VMEM((512, 32), F32),
            pltpu.VMEM((2, 32, L), F32),
            pltpu.VMEM((512, 32), F32),
            pltpu.VMEM((32, 2048), BF16),
            pltpu.VMEM((128, 512), BF16),
            pltpu.VMEM((8, 32), F32),
            pltpu.VMEM((8, 2048), F32),
            pltpu.VMEM((NZ, 16, 2048), BF16),
            pltpu.VMEM((NZ, 16, 2048), BF16),
            pltpu.VMEM((1, 1, 2048), F32),
            pltpu.VMEM((NZ, 1, 2048), F32),
            pltpu.VMEM((16, 2048), BF16),
            pltpu.VMEM((16, 2048), BF16),
            pltpu.VMEM((NZ, 16, 2048), BF16),
            pltpu.VMEM((NZ, 16, 2048), BF16),
            pltpu.VMEM((32, 16, P_SIZE), F32),
            pltpu.SemaphoreType.DMA((9,)),
            *GATHER_SEMS,
            *SCAN_SEMS,
            pltpu.SemaphoreType.DMA((NZ,)),
            pltpu.SemaphoreType.DMA((NZ,)),
        ],
        compiler_params=pltpu.CompilerParams(
            collective_id=0, has_side_effects=True, vmem_limit_bytes=46 << 20
        ),
    )(
        *[
            pltpu.with_memory_space_constraint(operand, pltpu.HBM)
            for operand in (
                out_weight.reshape(16, 128, 256),
                values[0],
                gate_values[0],
                prompt_state.transpose(0, 2, 1),
                state_in[0],
                state_out[0],
                step_size[0].T,
                log_decay[0].T,
                skip_gain.reshape(1, 32),
                norm_gain.reshape(1, 2048),
            )
        ]
    )
    return out[None]


def solution(mesh):
    split = Mesh(mesh.devices.reshape(2, 4, 2, NZ, 2), ("ylo", "x", "yhi", "z", "head"))
    return jax.shard_map(
        shards,
        mesh=split,
        in_specs=(
            P(SAMPLE, SEQ, "head"),
            P(SAMPLE, SEQ, "head"),
            P(SAMPLE, SEQ, None),
            P(SAMPLE, SEQ, None),
            P(SAMPLE, SEQ, "head"),
            P(SAMPLE, SEQ, "head"),
            P("head"),
            P("head"),
            P("head", SEQ),
            P("head", None, SAMPLE),
        ),
        out_specs=P(SAMPLE, SEQ, "head"),
        check_vma=False,
    )
```

```python
from functools import partial

import jax
import jax.numpy as jnp
from jax import lax
from jax.experimental import pallas as pl
from jax.experimental.pallas import tpu as pltpu
from jax.sharding import Mesh
from jax.sharding import PartitionSpec as P

P_SIZE = 64
L = 256
GROUP_HEADS = 8
SEQ = ("yhi", "z")
SAMPLE = ("ylo", "x")
NZ = 8
MESH_ID = pl.DeviceIdType.MESH
EPSILON = 1e-05


def place():
    names = ("ylo", "x", "yhi", "z", "head")
    at = {name: lax.axis_index(name) for name in names}
    y = at["yhi"] * 2 + at["ylo"]
    up, down = lax.rem(y + 1, 4), lax.rem(y + 3, 4)
    near = {
        "+x": {"x": lax.rem(at["x"] + 1, 4)},
        "-x": {"x": lax.rem(at["x"] + 3, 4)},
        "+y": {"yhi": up // 2, "ylo": lax.rem(up, 2)},
        "-y": {"yhi": down // 2, "ylo": lax.rem(down, 2)},
        "+z": {"z": lax.rem(at["z"] + 1, NZ)},
        "-z": {"z": lax.rem(at["z"] + NZ - 1, NZ)},
        "across": {"yhi": 1 - at["yhi"], "ylo": 1 - at["ylo"]},
        "beside": {"ylo": 1 - at["ylo"]},
        "sibling": {"head": 1 - at["head"]},
    }
    return at, near


WAYS = ("+x", "-x", "+y", "-y")


class Gather:
    def __init__(self, at, near, own, wbuf, sems):
        self.at, self.near, self.own, self.wbuf = at, near, own, wbuf
        self.zs, self.zr, self.fs, self.fr, self.gs, self.gr, self.ls = sems
        px, lo = lax.rem(at["x"], 2), at["ylo"]
        self.mine = px * 2 + lo
        self.byx = (1 - px) * 2 + lo
        self.byy = px * 2 + 1 - lo
        self.px = px
        self.s_own = at["yhi"] * NZ + at["z"]
        self.s_across = (1 - at["yhi"]) * NZ + at["z"]

    def copy(self, src, s, start, size, send, recv, to):
        dst = self.wbuf.at[s, pl.ds(start, size)]
        return pltpu.make_async_remote_copy(
            src_ref=dst if src is None else src,
            dst_ref=dst,
            send_sem=send,
            recv_sem=recv,
            device_id=self.near[to],
            device_id_type=MESH_ID,
        )

    def shard(self, fam, z):
        hi = self.at["yhi"] if fam == 0 else 1 - self.at["yhi"]
        return hi * NZ + lax.rem(z + 2 * NZ, NZ)

    def events(self, n):
        fam, k = n % 2, n // 2
        found = []
        if k < (4 if fam == 0 else 3):
            found.append((self.shard(fam, self.at["z"] - 1 - k), k, "+z"))
        if k < (3 if fam == 0 else 4):
            found.append((self.shard(fam, self.at["z"] + 1 + k), k, "-z"))
        return fam, found

    def ring(self, s, way, half, slot, own=False):
        start = self.mine * 4 + 2 * half
        src = self.own.at[pl.ds(start, 2)] if own else None
        return self.copy(src, s, start, 2, self.zs.at[slot, half], self.zr.at[s, half], way)

    def local(self):
        return pltpu.make_async_copy(self.own, self.wbuf.at[self.s_own], self.ls)

    def give(self, half):
        start = self.byy * 4 + 2 * half
        src = self.own.at[pl.ds(start, 2)]
        to = self.zr.at[self.s_own, half]
        return self.copy(src, self.s_own, start, 2, self.zs.at[0, half], to, "across")

    def given(self, half):
        to = self.zr.at[self.s_across, half]
        start = self.mine * 4 + 2 * half
        return self.copy(None, self.s_across, start, 2, self.zs.at[0, half], to, "across")

    def lend(self):
        to = self.fr.at[self.s_across, 2]
        return self.copy(None, self.s_across, self.mine * 4, 4, self.zs.at[16, 0], to, "beside")

    def lent(self):
        to = self.fr.at[self.s_across, 2]
        return self.copy(None, self.s_across, self.byy * 4, 4, self.zs.at[16, 0], to, "beside")

    def give_on(self, d):
        start = (self.mine if d == 0 else self.byy) * 4
        return self.copy(
            None, self.s_across, start, 4, self.fs.at[0, d], self.fr.at[self.s_across, d], WAYS[d]
        )

    def given_on(self, d):
        start = (self.byx if d == 0 else 3 - self.mine) * 4
        return self.copy(
            None, self.s_across, start, 4, self.fs.at[0, d], self.fr.at[self.s_across, d], WAYS[d]
        )

    def first(self, s, d, slot):
        start = self.mine * 4 + 2 * (d % 2)
        return self.copy(None, s, start, 2, self.fs.at[slot, d], self.fr.at[s, d], WAYS[d])

    def first_in(self, s, d):
        start = (self.byx if d < 2 else self.byy) * 4 + 2 * (d % 2)
        return self.copy(None, s, start, 2, self.fs.at[0, d], self.fr.at[s, d], WAYS[d])

    def second(self, s, d, slot):
        start = (self.byy if d < 2 else self.byx) * 4 + (0, 2, 1, 3)[d]
        return self.copy(None, s, start, 1, self.gs.at[slot, d], self.gr.at[s, d], WAYS[d])

    def second_in(self, s, d):
        far = 3 - self.mine
        start = far * 4 + (0, 2, 1, 3)[d]
        return self.copy(None, s, start, 1, self.gs.at[0, d], self.gr.at[s, d], WAYS[d])

    def send(self, *copies):
        for c in copies:
            c.start()
            self.sent.append(c)

    def begin(self):
        self.sent = []
        for i in range(2):
            self.send(
                self.ring(self.s_own, "+z", i, 1, True),
                self.ring(self.s_own, "-z", 1 - i, 2, True),
                self.give(i),
            )
        self.local().start()
        self.slots = {"z": 5, "f": 1, "g": 0}

    def begin_across(self):
        for i in range(2):
            self.given(i).wait_recv()
            self.send(
                self.ring(self.s_across, "+z", i, 3),
                self.ring(self.s_across, "-z", i, 4),
            )
        self.send(self.give_on(0), self.lend())

    def go_on_across(self):
        self.lent().wait_recv()
        c = self.give_on(1)
        c.start()
        self.sent.append(c)

    def forward(self, n):
        fam, found = self.events(n)
        slots = [(self.slots["z"] + i, self.slots["f"] + i) for i in range(len(found))]
        self.slots["f"] += len(found)
        for i in range(2):
            for (s, k, way), (zslot, fslot) in zip(found, slots):
                half = i if way == "+z" or fam == 1 else 1 - i
                self.ring(s, way, half, 0).wait_recv()
                last = k + 1 == (4 if (fam == 0) == (way == "+z") else 3)
                if not last:
                    self.send(self.ring(s, way, half, zslot))
                self.send(self.first(s, half, fslot), self.first(s, 2 + half, fslot))
        for s, k, way in found:
            last = k + 1 == (4 if (fam == 0) == (way == "+z") else 3)
            if not last:
                self.slots["z"] += 1

    def spread(self, n):
        fam, found = self.events(n)
        for s, k, way in found:
            for d in (2, 3, 0, 1):
                self.first_in(s, d).wait_recv()
                c = self.second(s, (d + 2) % 4, self.slots["g"])
                c.start()
                self.sent.append(c)
            self.slots["g"] += 1

    def arrived(self, n):
        fam, found = self.events(n)
        for s, k, way in found:
            for d in range(4):
                self.second_in(s, d).wait_recv()

    def arrived_across(self):
        self.local().wait()
        for d in range(2):
            self.given_on(d).wait_recv()

    def finish(self):
        for c in self.sent:
            c.wait_send()


def greet(at, near):
    barrier = pltpu.get_barrier_semaphore()
    who = [near["across"], near["sibling"], {"yhi": 1 - at["yhi"]}]
    who += [near_z(at, k) for k in range(1, NZ)]
    who += [near_sample(at, k) for k in range(1, 8)]
    for device in who:
        pl.semaphore_signal(barrier, inc=1, device_id=device, device_id_type=MESH_ID)
    pl.semaphore_wait(barrier, len(who))


def near_z(at, k):
    return {"z": lax.rem(at["z"] + k, NZ)}


def near_sample(at, k):
    ylo = at["ylo"] if k < 4 else 1 - at["ylo"]
    return {"ylo": ylo, "x": lax.rem(at["x"] + k % 4, 4)}


GATHER_SEMS = [
    pltpu.SemaphoreType.DMA((17, 2)),
    pltpu.SemaphoreType.DMA((16, 2)),
    pltpu.SemaphoreType.DMA((15, 4)),
    pltpu.SemaphoreType.DMA((16, 4)),
    pltpu.SemaphoreType.DMA((14, 4)),
    pltpu.SemaphoreType.DMA((16, 4)),
    pltpu.SemaphoreType.DMA,
]


class Project:
    def __init__(self, at, near, normed, wbuf, part, got, out, sems):
        self.at, self.near, self.normed, self.wbuf = at, near, normed, wbuf
        self.part, self.got, self.out, self.ss, self.rs = part, got, out, *sems

    def dot(self, s):
        w = self.wbuf[s].reshape(2048, 256)
        return jnp.dot(self.normed[...], w, preferred_element_type=jnp.float32).astype(jnp.bfloat16)

    def copy(self, z):
        return pltpu.make_async_remote_copy(
            src_ref=self.part.at[1, z],
            dst_ref=self.got.at[z],
            send_sem=self.ss.at[z],
            recv_sem=self.rs.at[z],
            device_id=self.near["sibling"],
            device_id_type=MESH_ID,
        )

    def columns(self, z):
        c = self.at["head"]
        self.part[1, z] = self.dot((1 - c) * NZ + z)
        self.copy(z).start()
        self.part[0, z] = self.dot(c * NZ + z)

    def combine(self, z):
        self.copy(z).wait_recv()
        total = self.part[0, z].astype(jnp.float32) + self.got[z].astype(jnp.float32)
        start = pl.multiple_of(z * 256, 256)
        self.out[:, pl.ds(start, 256)] = total.astype(jnp.bfloat16)


F32, BF16 = jnp.float32, jnp.bfloat16


def mm(a, b):
    return jnp.dot(a, b, preferred_element_type=F32)


def nt(a, b):
    return lax.dot_general(a, b, (((1,), (1,)), ((), ())), preferred_element_type=F32)


def three(v):
    a = v.astype(BF16)
    rest = v - a.astype(F32)
    b = rest.astype(BF16)
    return a, b, (rest - b.astype(F32)).astype(BF16)


def by_column(v, e):
    return mm(jnp.concatenate(three(v), axis=1), e)


def iota(shape, dim):
    return lax.broadcasted_iota(jnp.int32, shape, dim)


def remote(src, dst, send, recv, to):
    return pltpu.make_async_remote_copy(
        src_ref=src,
        dst_ref=dst,
        send_sem=send,
        recv_sem=recv,
        device_id=to,
        device_id_type=MESH_ID,
    )


class Scan:
    def __init__(self, at, sout, sin, dsend, din, init, tsend, eout, entry, sems):
        self.at = at
        self.sout, self.sin, self.dsend, self.din = sout, sin, dsend, din
        self.init, self.tsend, self.eout, self.entry = init, tsend, eout, entry
        self.ss, self.sr, self.ds, self.dr, self.es, self.er, self.ps, self.ir, self.ts = sems

    def peer(self, k):
        return lax.rem(self.at["z"] + k, NZ)

    def state(self, k):
        z, to = self.at["z"], self.peer(k)
        return remote(self.sout.at[to], self.sin.at[z], self.ss.at[k], self.sr.at[z], {"z": to})

    def state_in(self, k):
        z = self.peer(k)
        return remote(self.sout.at[z], self.sin.at[z], self.ss.at[k], self.sr.at[z], {"z": z})

    def decay(self, k):
        z, to = self.at["z"], self.peer(k)
        return remote(self.dsend.at[0], self.din.at[z], self.ds.at[k], self.dr.at[z], {"z": to})

    def decay_in(self, k):
        z = self.peer(k)
        return remote(self.dsend.at[0], self.din.at[z], self.ds.at[k], self.dr.at[z], {"z": z})

    def entering(self, k):
        z, to = self.at["z"], self.peer(k)
        return remote(self.eout.at[to], self.entry.at[z], self.es.at[k], self.er.at[z], {"z": to})

    def entering_in(self, k):
        z = self.peer(k)
        return remote(self.eout.at[z], self.entry.at[z], self.es.at[k], self.er.at[z], {"z": z})

    def prompt(self, k):
        return remote(
            self.tsend, self.init, self.ps.at[k], self.ir, near_sample(self.at, k)
        )

    def total(self):
        return remote(self.tsend, self.init, self.ts, self.ir, {"yhi": 1 - self.at["yhi"]})

    def holds_prompt(self):
        m = self.at["ylo"] * 4 + self.at["x"]
        return (m == self.at["z"]) & (self.at["yhi"] == 0)

    def send_prompt(self, prompt_hbm, prompt_vmem, sem):
        @pl.when(self.holds_prompt())
        def _():
            load = pltpu.make_async_copy(prompt_hbm, prompt_vmem, sem)
            load.start()
            load.wait()
            for j in range(0, 32, 2):
                two = jnp.concatenate([prompt_vmem[j], prompt_vmem[j + 1]], axis=1).astype(BF16)
                self.tsend[:, j * P_SIZE : (j + 2) * P_SIZE] = two
                self.init[:, j * P_SIZE : (j + 2) * P_SIZE] = two
            for k in range(1, 8):
                self.prompt(k).start()

    def send_states(self):
        for k in range(1, NZ):
            self.state(k).start()
            self.decay(k).start()
        z = self.at["z"]
        self.sin[z] = self.sout[z]
        self.din[z] = self.dsend[0]

    def combine(self, hi):
        @pl.when(self.at["yhi"] == hi)
        def _():
            for k in range(1, NZ):
                self.state_in(k).wait_recv()
                self.decay_in(k).wait_recv()
            if hi == 0:
                @pl.when(self.holds_prompt())
                def _():
                    for k in range(1, 8):
                        self.prompt(k).wait_send()

                @pl.when(jnp.logical_not(self.holds_prompt()))
                def _():
                    self.prompt(1).wait_recv()
            else:
                self.total().wait_recv()

            def step(j, acc):
                self.eout[j] = acc.astype(BF16)
                return acc * self.din[j] + self.sin[j].astype(F32)

            acc = lax.fori_loop(0, NZ, step, self.init[...].astype(F32))
            if hi == 0:
                self.tsend[...] = acc.astype(BF16)
                self.total().start()
            for k in range(1, NZ):
                self.entering(k).start()
            z = self.at["z"]
            self.entry[z] = self.eout[z]

    def entered(self):
        for k in range(1, NZ):
            self.entering_in(k).wait_recv()

    def finish(self):
        for k in range(1, NZ):
            self.state(k).wait_send()
            self.decay(k).wait_send()
            self.entering(k).wait_send()

        @pl.when(self.at["yhi"] == 0)
        def _():
            self.total().wait_send()


SCAN_SEMS = [pltpu.SemaphoreType.DMA((NZ,))] * 7 + [pltpu.SemaphoreType.DMA] * 2


class Local:
    def __init__(self, **refs):
        self.__dict__.update(refs)

    def prepare(self):
        picks = iota((32, 2048), 0) == lax.shift_right_logical(iota((32, 2048), 1), 6)
        self.e[...] = jnp.concatenate([picks.astype(F32)] * 3, axis=0).astype(BF16)
        tri = (iota((L, L), 0) >= iota((L, L), 1)).astype(F32).astype(BF16)
        eye = (iota((L, L), 0) == iota((L, L), 1)).astype(F32).astype(BF16)
        small = (iota((32, 32), 0) == iota((32, 32), 1)).astype(F32).astype(BF16)
        self.bt[...] = self.b_in[...].astype(F32).T.astype(BF16)
        for b in range(2):
            rows = slice(b * L, b * L + L)
            a, m, c = [nt(tri, part) for part in three(self.log_decay[:, rows])]
            run = a + m + c
            self.run[rows] = run
            a, m, c = [nt(small, part) for part in three(run)]
            self.runt[b] = a + m + c
            a, m, c = [nt(eye, part) for part in three(self.step[:, rows])]
            self.stept[rows] = a + m + c
            self.scores[b] = mm(self.c_out[rows], self.bt[:, rows])
        ends = [self.run[L - 1 : L], self.run[2 * L - 1 : 2 * L]]
        line = iota((8, 32), 0)
        self.lines[...] = jnp.where(
            line == 0,
            jnp.exp(ends[0]),
            jnp.where(
                line == 1,
                jnp.exp(ends[1]),
                jnp.where(line == 2, jnp.exp(ends[0] + ends[1]), self.skip_gain[...]),
            ),
        )

    def states(self, lo, hi):
        def group(g, _):
            cols = pl.ds(pl.multiple_of(g * 512, 512), 512)
            e = self.e[:, cols]
            wide = by_column(self.lines[...], e)
            self.wide[:, cols] = wide
            self.dsend[0, :, cols] = wide[2:3]
            found = []
            for b in range(2):
                rows = slice(b * L, b * L + L)
                run = self.run[rows]
                self.re[rows, cols] = by_column(run, e)
                scaled = (self.values[rows, cols].astype(F32) * by_column(self.stept[rows], e)).astype(BF16)
                self.scaled[rows, cols] = scaled
                tail = by_column(jnp.exp(run[L - 1 : L] - run), e)
                weighted = (scaled.astype(F32) * tail).astype(BF16)
                found.append(mm(self.bt[:, rows], weighted))
            self.bs0[:, cols] = found[0]
            state = (wide[1:2] * found[0] + found[1]).astype(BF16)
            self.sout[:, :, cols] = state.reshape(NZ, 16, 512)
            return 0

        lax.fori_loop(lo, hi, group, 0)

    def mix(self, b, lo, hi):
        half = L // 2
        keep = iota((half, half), 0) >= iota((half, half), 1)
        first = iota((L, 128), 1) < P_SIZE
        rows = slice(b * L, b * L + L)

        def pair(j, _):
            cols = pl.ds(pl.multiple_of(j * 128, 128), 128)
            scaled = self.scaled[rows, cols]
            re = self.re[rows, cols]
            made = []
            for one in range(2):
                col = re[:, one * P_SIZE : one * P_SIZE + 1]
                row = self.runt[b, pl.ds(2 * j + one, 1), :]
                top = jnp.exp(jnp.where(keep, col[:half] - row[:, :half], -1e30))
                top = (self.scores[b, :half, :half] * top).astype(BF16)
                left = jnp.exp(col[half:] - row[:, :half])
                left = (self.scores[b, half:, :half] * left).astype(BF16)
                right = jnp.exp(jnp.where(keep, col[half:] - row[:, half:], -1e30))
                right = (self.scores[b, half:, half:] * right).astype(BF16)
                under = mm(jnp.concatenate([left, right], axis=1), scaled)
                made.append(jnp.concatenate([mm(top, scaled[:half]), under], axis=0))
            self.lout[rows, cols] = jnp.where(first, made[0], made[1])
            return 0

        lax.fori_loop(lo, hi, pair, 0)

    def normalize(self, b, lo, hi):
        def group(g, _):
            cols = pl.ds(pl.multiple_of(g * 512, 512), 512)
            start = self.entry[:, :, cols].reshape(128, 512)
            if b == 1:
                start = (self.wide[0:1, cols] * start.astype(F32) + self.bs0[:, cols]).astype(BF16)
            for r in range(b * L, b * L + L, 128):
                rows = slice(r, r + 128)
                carried = jnp.exp(self.re[rows, cols]) * mm(self.c_out[rows], start)
                out = self.lout[rows, cols] + self.wide[3:4, cols] * self.values[rows, cols].astype(F32)
                out = out + carried
                v = self.gate[rows, cols].astype(F32)
                gated = out * (0.5 * v * (1.0 + jnp.tanh(0.5 * v)))
                mean = jnp.sum(gated * gated, axis=1, keepdims=True) * (1.0 / 512)
                scaled = gated * lax.rsqrt(mean + EPSILON) * self.norm_gain[:, cols]
                self.normed[rows, cols] = scaled.astype(BF16)
            return 0

        lax.fori_loop(lo, hi, group, 0)


ORDER = (
    ("gate",), ("s", 3, 4), ("s", 0, 1), ("across",), ("s", 1, 2), ("s", 2, 3), ("z", 0), ("z", 1),
    ("m", 1, 12, 16), ("send",), ("z", 2), ("across2",), ("m", 1, 0, 4), ("m", 1, 8, 12), ("m", 1, 4, 8), ("z", 3),
    ("m", 0, 12, 16), ("m", 0, 4, 8), ("x", 2), ("x", 0), ("across3",), ("x", 1), ("scan", 0), ("x", 3),
    ("scan", 1), ("r", 0), ("m", 0, 8, 12), ("z", 4), ("z", 5), ("r", 1), ("m", 0, 0, 4), ("x", 4), ("entered",),
    ("n", 0, 0, 4), ("r", 3), ("x", 5), ("r", 2), ("n", 1, 0, 4), ("z", 7), ("c", 1), ("z", 6), ("c", 2), ("c", 0),
    ("x", 7), ("r", 4), ("o", 1), ("x", 6), ("r", 5), ("c", 3), ("o", 0), ("o", 2), ("r", 6), ("r", 7), ("c", 4),
    ("o", 3), ("o", 4),
)


def kernel(
    own, values_hbm, gate_hbm, prompt_hbm, b_hbm, c_hbm, step_hbm, decay_hbm, skip_hbm, norm_hbm,
    result, b_in, c_out, step, log_decay, skip_gain, norm_gain,
    wbuf, part, got, values, gate, scaled, re, lout, bs0, scores, run, runt, stept, e, bt,
    lines, wide, sout, sin, dsend, din, init, tsend, eout, entry, prompt, load, *sems,
):
    at, near = place()
    normed = scaled
    pairs = (
        (decay_hbm, log_decay), (step_hbm, step), (b_hbm, b_in), (c_hbm, c_out), (skip_hbm, skip_gain),
        (values_hbm, values), (norm_hbm, norm_gain), (gate_hbm, gate),
    )
    loads = [pltpu.make_async_copy(src, dst, load.at[i]) for i, (src, dst) in enumerate(pairs)]
    for copy in loads:
        copy.start()
    greet(at, near)
    gather = Gather(at, near, own, wbuf, sems[:7])
    scan = Scan(at, sout, sin, dsend, din, init, tsend, eout, entry, sems[7:16])
    proj = Project(at, near, normed, wbuf, part, got, result, sems[16:18])
    local = Local(
        b_in=b_in, c_out=c_out, step=step, log_decay=log_decay, skip_gain=skip_gain, norm_gain=norm_gain,
        values=values, gate=gate, scaled=scaled, re=re, lout=lout, normed=normed, bs0=bs0, scores=scores,
        run=run, runt=runt, stept=stept, e=e, bt=bt, lines=lines, wide=wide, sout=sout, dsend=dsend, entry=entry,
    )
    z = at["z"]

    def columns(k):
        proj.columns(lax.rem(z + k, NZ))
        if 0 < k < 4:
            proj.columns(lax.rem(z + NZ - k, NZ))

    def combine(k):
        proj.combine(lax.rem(z + k, NZ))
        if 0 < k < 4:
            proj.combine(lax.rem(z + NZ - k, NZ))

    steps = {
        "z": gather.forward,
        "x": gather.spread,
        "r": gather.arrived,
        "s": local.states,
        "m": local.mix,
        "n": local.normalize,
        "c": columns,
        "o": combine,
        "across": gather.begin_across,
        "across2": gather.go_on_across,
        "across3": gather.arrived_across,
        "scan": scan.combine,
        "send": scan.send_states,
        "entered": scan.entered,
        "gate": lambda: (loads[6].wait(), loads[7].wait()),
    }
    gather.begin()
    scan.send_prompt(prompt_hbm, prompt, load.at[8])
    for copy in loads[:5]:
        copy.wait()
    local.prepare()
    loads[5].wait()
    for what, *how in ORDER:
        steps[what](*how)
    for k in range(NZ):
        proj.copy(k).wait_send()
    scan.finish()
    gather.finish()


def shards(
    values,
    gate_values,
    state_in,
    state_out,
    step_size,
    log_decay,
    skip_gain,
    norm_gain,
    out_weight,
    prompt_state,
):
    vmem = pl.BlockSpec(memory_space=pltpu.VMEM)
    hbm = pl.BlockSpec(memory_space=pltpu.HBM)
    out = pl.pallas_call(
        kernel,
        name="layer",
        out_shape=jax.ShapeDtypeStruct((512, 2048), BF16),
        in_specs=[hbm] * 10,
        out_specs=vmem,
        scratch_shapes=[
            pltpu.VMEM((512, 128), BF16),
            pltpu.VMEM((512, 128), BF16),
            pltpu.VMEM((32, 512), F32),
            pltpu.VMEM((32, 512), F32),
            pltpu.VMEM((1, 32), F32),
            pltpu.VMEM((1, 2048), F32),
            pltpu.VMEM((16, 16, 128, 256), BF16),
            pltpu.VMEM((2, NZ, 512, 256), BF16),
            pltpu.VMEM((NZ, 512, 256), BF16),
            pltpu.VMEM((512, 2048), BF16),
            pltpu.VMEM((512, 2048), BF16),
            pltpu.VMEM((512, 2048), BF16),
            pltpu.VMEM((512, 2048), F32),
            pltpu.VMEM((512, 2048), F32),
            pltpu.VMEM((128, 2048), F32),
            pltpu.VMEM((2, L, L), F32),
            pltpu.VMEM((512, 32), F32),
            pltpu.VMEM((2, 32, L), F32),
            pltpu.VMEM((512, 32), F32),
            pltpu.VMEM((96, 2048), BF16),
            pltpu.VMEM((128, 512), BF16),
            pltpu.VMEM((8, 32), F32),
            pltpu.VMEM((8, 2048), F32),
            pltpu.VMEM((NZ, 16, 2048), BF16),
            pltpu.VMEM((NZ, 16, 2048), BF16),
            pltpu.VMEM((1, 1, 2048), F32),
            pltpu.VMEM((NZ, 1, 2048), F32),
            pltpu.VMEM((16, 2048), BF16),
            pltpu.VMEM((16, 2048), BF16),
            pltpu.VMEM((NZ, 16, 2048), BF16),
            pltpu.VMEM((NZ, 16, 2048), BF16),
            pltpu.VMEM((32, 16, P_SIZE), F32),
            pltpu.SemaphoreType.DMA((9,)),
            *GATHER_SEMS,
            *SCAN_SEMS,
            pltpu.SemaphoreType.DMA((NZ,)),
            pltpu.SemaphoreType.DMA((NZ,)),
        ],
        compiler_params=pltpu.CompilerParams(
            collective_id=0, has_side_effects=True, vmem_limit_bytes=46 << 20
        ),
    )(
        *[
            pltpu.with_memory_space_constraint(operand, pltpu.HBM)
            for operand in (
                out_weight.reshape(16, 128, 256),
                values[0],
                gate_values[0],
                prompt_state.transpose(0, 2, 1),
                state_in[0],
                state_out[0],
                step_size[0].T,
                log_decay[0].T,
                skip_gain.reshape(1, 32),
                norm_gain.reshape(1, 2048),
            )
        ]
    )
    return out[None]


def solution(mesh):
    split = Mesh(mesh.devices.reshape(2, 4, 2, NZ, 2), ("ylo", "x", "yhi", "z", "head"))
    return jax.shard_map(
        shards,
        mesh=split,
        in_specs=(
            P(SAMPLE, SEQ, "head"),
            P(SAMPLE, SEQ, "head"),
            P(SAMPLE, SEQ, None),
            P(SAMPLE, SEQ, None),
            P(SAMPLE, SEQ, "head"),
            P(SAMPLE, SEQ, "head"),
            P("head"),
            P("head"),
            P("head", SEQ),
            P("head", None, SAMPLE),
        ),
        out_specs=P(SAMPLE, SEQ, "head"),
        check_vma=False,
    )
```
